32 devices in a mesh: view: 4 (over x, core), samp: 8 (over z, y).
Axes of the slice: x: 2, y: 2, z: 4, core: 2. Of those that a mesh axis runs over, the one named last changes fastest.
Arguments:
- view_data: bfloat16 [8, 4096, 2048], P('view', 'samp'), may hold values from -10 to 10
- init_coeffs: float32 [8, 2048, 128], P('view'), may hold values from -0.125 to 0.125
Outputs:
- shared_scores: float32 [4096, 128], P('samp')
- final_coeffs: float32 [8, 2048, 128], P('view', 'samp')
The draws below stay inside these ranges and needn't reach their ends.
All inputs are finite; a program needn't handle non-finite values.
Results may differ from the reference program's by a relative error of at most 0.005.
Values may be sent and summed in bfloat16 or wider, within the bound.
No kernel may reach another device: no remote copies, remote signals or barrier semaphores. Data moves between devices by JAX's collectives and lax.ppermute only.
A program may use at most 128 MiB of HBM per device.

```python
import jax
import jax.numpy as jnp
from jax import lax

F = 2048
K = 128
OUTER = 2
INNER = 2
NS_ITERS = 12
VIEWS = 8
NSAMP = 4096


def draw_view_data(key, part):
    key_feat = jax.random.fold_in(key, 11)
    key_noise = jax.random.fold_in(key, 23)
    top = 10.0
    feat = jax.random.uniform(key_feat, (VIEWS, 1, F), jnp.float32)
    where = (jnp.arange(NSAMP, dtype=jnp.float32) + 0.5) / NSAMP
    rate = 2.0 * jnp.log(top) * feat
    safe_rate = jnp.maximum(rate, 0.0001)
    mean_square = jnp.where(rate > 0.0001, jnp.expm1(safe_rate) / safe_rate, 1.0 + 0.5 * rate)
    growth = jnp.exp(0.5 * rate * where[None, :, None]) / jnp.sqrt(mean_square)
    noise = jnp.clip(jax.random.normal(key_noise, (VIEWS, NSAMP, F), jnp.float32), -4.0, 4.0)
    return (noise * growth).astype(jnp.bfloat16)


def shard_levels(rng, dims, split, low, top_value):
    factor_of, own = 1.0, jax.random.fold_in(rng, 6)
    for dim, blocks in split:
        draws = jnp.exp(jax.random.uniform(jax.random.fold_in(own, dim), (blocks,), jnp.float32, low / len(split), top_value / len(split)))
        factor_of = factor_of * jnp.repeat(draws, dims[dim] // blocks).reshape([-1 if axis == dim else 1 for axis in range(len(dims))])
    return factor_of


def gaussian(stream_key, shape, spread, most, cuts=(), held_as=jnp.bfloat16):
    result = jax.random.normal(stream_key, shape, jnp.float32) * spread
    if len(cuts) > 0:
        result = shard_levels(stream_key, shape, cuts, -0.22, 0.18) * result
    return jnp.clip(result, min=-most, max=most).astype(held_as)


def setup_inputs(seed: int = 0) -> dict:
    splits = jax.random.split(jax.random.key(seed), 3)
    return {
        "view_data": draw_view_data(jax.random.fold_in(splits[2], 71), 0),
        "init_coeffs": gaussian(splits[1], (VIEWS, F, K), F ** -0.5, 0.125, ((0, 4),), jnp.float32),
    }


HIGH = lax.Precision.HIGHEST
ridge_weight = 0.1
step_size = 0.5

def newton_inverse(gram):
    size_k = gram.shape[0]
    eye_mat = jnp.eye(size_k, dtype=jnp.float32)
    shrunk = gram + jnp.trace(gram) / size_k * eye_mat
    scale = jnp.sqrt(jnp.sum(shrunk * shrunk))
    approx = shrunk / scale
    inverse = eye_mat
    for turn in range(NS_ITERS):
        factor = 0.5 * (3.0 * eye_mat - jnp.dot(inverse, approx, precision=HIGH))
        approx = jnp.dot(approx, factor, precision=HIGH)
        inverse = jnp.dot(factor, inverse, precision=HIGH)
    return (inverse, scale)

def make_scores(view_data, coeffs):
    summed = jnp.zeros((view_data.shape[1], coeffs.shape[2]), jnp.float32)
    for member in range(view_data.shape[0]):
        summed = summed + jnp.dot(view_data[member], coeffs[member].astype(jnp.bfloat16), preferred_element_type=jnp.float32)
    gram = jnp.dot(summed.T, summed, precision=HIGH)
    inverse, scale = newton_inverse(gram)
    return jnp.dot(summed, inverse, precision=HIGH) * jnp.sqrt(view_data.shape[1] / scale)

def reference(view_data, init_coeffs):
    total = view_data.shape[1]
    coeffs = init_coeffs
    scores = make_scores(view_data, coeffs)
    for outer_step in range(OUTER):
        for inner_step in range(INNER):
            updated = []
            for member in range(view_data.shape[0]):
                weights = coeffs[member]
                resid = (jnp.dot(view_data[member], weights.astype(jnp.bfloat16), preferred_element_type=jnp.float32) - scores).astype(jnp.bfloat16)
                term = lax.dot_general(view_data[member], resid, (((0,), (0,)), ((), ())), preferred_element_type=jnp.float32)
                grad = term / total + ridge_weight * weights
                updated.append(weights - step_size * grad)
            coeffs = jnp.stack(updated)
        scores = make_scores(view_data, coeffs)
    return (scores, coeffs)
```

```python
import jax
import jax.numpy as jnp
from jax import lax
from jax.sharding import PartitionSpec as P

OUTER = 2
INNER = 2
NS_ITERS = 12

HIGH = lax.Precision.HIGHEST
ridge_weight = 0.1
step_size = 0.5
AXES = ("view", "samp")
GROUP = 4


def newton_inverse(gram):
    size_k = gram.shape[0]
    eye_mat = jnp.eye(size_k, dtype=jnp.float32)
    shrunk = gram + jnp.trace(gram) / size_k * eye_mat
    scale = jnp.sqrt(jnp.sum(shrunk * shrunk))
    approx = shrunk / scale
    inverse = eye_mat
    for turn in range(NS_ITERS):
        factor = 0.5 * (3.0 * eye_mat - jnp.dot(inverse, approx, precision=HIGH))
        approx = jnp.dot(approx, factor, precision=HIGH)
        inverse = jnp.dot(factor, inverse, precision=HIGH)
    return (inverse, scale)


class Grid:
    def __init__(self, n_view, n_samp):
        self.planes, self.squares = n_view // 2, n_samp // GROUP
        self.n_samp = n_samp

    def encode(self, plane, core, square, corner):
        return (plane * 2 + core) * self.n_samp + square * GROUP + corner

    def each(self):
        for plane in range(self.planes):
            for core in range(2):
                for square in range(self.squares):
                    for corner in range(GROUP):
                        yield plane, core, square, corner

    def permute(self, value, target):
        pairs = [(self.encode(*at), self.encode(*target(*at))) for at in self.each()]
        return lax.ppermute(value, AXES, pairs)

    def swap_core(self, value):
        return self.permute(value, lambda a, c, q, p: (a, 1 - c, q, p))

    def sum_squares(self, value, wire):
        bit = 1
        while bit < self.squares:
            low = value.astype(wire)
            other = self.permute(low, lambda a, c, q, p, bit=bit: (a, c, q ^ bit, p))
            value = low.astype(jnp.float32) + other.astype(jnp.float32)
            bit *= 2
        return value

    def sum_planes(self, value):
        bit = 1
        while bit < self.planes:
            value = value + self.permute(value, lambda a, c, q, p, bit=bit: (a ^ bit, c, q, p))
            bit *= 2
        return value


def pick(parts, index):
    return lax.dynamic_index_in_dim(parts, index, 0, keepdims=False)


def body(view_data, init_coeffs):
    low = jnp.bfloat16
    grid = Grid(lax.axis_size("view"), lax.axis_size("samp"))
    rows, feats = view_data.shape[1:]
    comps = init_coeffs.shape[2]
    half_k, half_rows = comps // 2, rows // 2
    pooled = rows * GROUP
    total = rows * lax.axis_size("samp")
    view_at, samp_at = lax.axis_index("view"), lax.axis_index("samp")
    core = view_at % 2
    square, corner = samp_at // GROUP, samp_at % GROUP

    slots = []
    for k in range(GROUP):
        m = corner ^ k
        piece = lax.dynamic_slice(
            view_data, (m % 2, (m // 2) * half_rows, 0), (1, half_rows, feats)
        )[0]
        slots.append(
            grid.permute(
                piece,
                lambda a, c, q, p, k=k: (a, (p ^ k) // 2, q, 2 * c + (p ^ k) % 2),
            )
        )
    data = jnp.zeros((pooled, feats), low)
    for k in range(GROUP):
        source = (2 * core + corner % 2) ^ k
        other = grid.swap_core(slots[k])
        data = lax.dynamic_update_slice(data, slots[k], ((2 * source + core) * half_rows, 0))
        data = lax.dynamic_update_slice(
            data, other, ((2 * (source ^ 2) + 1 - core) * half_rows, 0)
        )

    local = jnp.transpose(pick(init_coeffs, corner % 2)).reshape(2, half_k, feats)
    from_core = grid.swap_core(pick(local, 1 - core))
    coeffs = jnp.where(core == corner // 2, pick(local, core), from_core)

    def whiten(pooled_sums):
        part = lax.dot_general(
            pooled_sums, pooled_sums, (((1,), (1,)), ((), ())), preferred_element_type=jnp.float32
        )
        gram = grid.sum_squares(part, jnp.float32)
        inverse, scale = newton_inverse(gram)
        return inverse * jnp.sqrt(total / scale)

    def half_scores(mixing, pooled_sums):
        own = lax.dynamic_slice_in_dim(mixing, core * half_k, half_k, 1)
        return lax.dot_general(
            own, pooled_sums.astype(jnp.float32), (((0,), (0,)), ((), ())), precision=HIGH
        )

    coeffs_low = init_coeffs.astype(low)
    part = jnp.zeros((comps, rows), jnp.float32)
    for member in range(view_data.shape[0]):
        part = part + lax.dot_general(
            coeffs_low[member],
            view_data[member],
            (((0,), (1,)), ((), ())),
            preferred_element_type=jnp.float32,
        )
    mine = lax.dynamic_slice_in_dim(part, core * half_rows, half_rows, 1)
    theirs = lax.dynamic_slice_in_dim(part, (1 - core) * half_rows, half_rows, 1)
    mine = grid.sum_planes(mine + grid.swap_core(theirs))
    square_groups = [
        [grid.encode(a, c, q, p) for p in range(GROUP) for c in range(2)]
        for a in range(grid.planes)
        for q in range(grid.squares)
    ]
    gathered = lax.all_to_all(
        jnp.broadcast_to(mine.astype(low), (2 * GROUP, comps, half_rows)),
        AXES, 0, 0, axis_index_groups=square_groups,
    )
    sums = jnp.transpose(gathered, (1, 0, 2)).reshape(comps, pooled)
    mixing = whiten(sums)
    scores = half_scores(mixing, sums)

    n_sub = GROUP * grid.planes
    sub = pooled // n_sub
    reduce_groups = [
        [grid.encode(a, c, q, p) for a in range(grid.planes) for p in range(GROUP)]
        for c in range(2)
        for q in range(grid.squares)
    ]
    gather_groups = [
        [
            grid.encode(a, c, q, p)
            for c in range(2)
            for a in range(grid.planes)
            for p in range(GROUP)
        ]
        for q in range(grid.squares)
    ]

    def product(weights):
        return lax.dot_general(
            weights.astype(low), data, (((1,), (1,)), ((), ())), preferred_element_type=jnp.float32
        )

    values = product(coeffs)
    for outer_step in range(OUTER):
        for inner_step in range(INNER):
            if inner_step > 0:
                values = product(coeffs)
            resid = (values - scores).astype(low)
            term = jnp.dot(resid, data, preferred_element_type=jnp.float32)
            grad = grid.sum_squares(term, low)
            coeffs = coeffs - step_size * (grad / total + ridge_weight * coeffs)
        values = product(coeffs)
        parts = jnp.transpose(values.astype(low).reshape(half_k, n_sub, sub), (1, 0, 2))
        parts = lax.all_to_all(parts, AXES, 0, 0, axis_index_groups=reduce_groups)
        own = jnp.sum(parts.astype(jnp.float32), axis=0).astype(low)
        gathered = lax.all_to_all(
            jnp.broadcast_to(own, (2 * n_sub, half_k, sub)),
            AXES, 0, 0, axis_index_groups=gather_groups,
        )
        sums = jnp.transpose(gathered.reshape(2, n_sub, half_k, sub), (0, 2, 1, 3)).reshape(
            comps, pooled
        )
        mixing = whiten(sums)
        if outer_step < OUTER - 1:
            scores = half_scores(mixing, sums)
    block = lax.dynamic_slice_in_dim(sums, corner * rows, rows, 1).astype(jnp.float32)
    shared = lax.dot_general(block, mixing, (((0,), (0,)), ((), ())), precision=HIGH)

    out_rows = feats // lax.axis_size("samp")
    pieces = []
    for k in range(GROUP):
        corner_to = (2 * core + corner % 2) ^ k
        piece = lax.dynamic_slice_in_dim(
            coeffs, (square * GROUP + corner_to) * out_rows, out_rows, 1
        )
        pieces.append(
            grid.permute(
                piece,
                lambda a, c, q, p, k=k: (a, p // 2, q, (2 * c + p % 2) ^ k),
            )
        )
    pieces = jnp.stack(pieces)
    ordered = [pick(pieces, corner ^ r) for r in range(GROUP)]
    final = jnp.stack(
        [jnp.concatenate([ordered[member], ordered[2 + member]], axis=0).T for member in range(2)]
    )
    return (shared, final)


def solution(mesh):
    in_specs = (P("view", "samp", None), P("view", None, None))
    out_specs = (P("samp", None), P("view", "samp", None))
    return jax.shard_map(body, mesh=mesh, in_specs=in_specs, out_specs=out_specs, check_vma=False)
```

```python
import jax
import jax.numpy as jnp
from jax import lax
from jax.experimental import pallas as pl
from jax.experimental.pallas import tpu as pltpu
from jax.sharding import PartitionSpec as P


OUTER = 2
INNER = 2
NS_ITERS = 12

ridge_weight = 0.1
step_size = 0.5
AXES = ("view", "samp")
GROUP = 4


def split(value):
    top = value.astype(jnp.bfloat16)
    return top, (value - top.astype(jnp.float32)).astype(jnp.bfloat16)


def fine_dot(left, right):
    left_top, left_rest = split(left)
    right_top, right_rest = split(right)
    out = jnp.dot(left_top, right_rest, preferred_element_type=jnp.float32)
    out = out + jnp.dot(left_rest, right_top, preferred_element_type=jnp.float32)
    return out + jnp.dot(left_top, right_top, preferred_element_type=jnp.float32)


def tall_dot(left, right):
    return lax.dot_general(left, right, (((1,), (1,)), ((), ())), preferred_element_type=jnp.float32)


def mixed_dot(mixing, sums):
    top, rest = split(mixing)
    return jnp.dot(rest, sums, preferred_element_type=jnp.float32) + jnp.dot(
        top, sums, preferred_element_type=jnp.float32
    )


def newton(total, gram):
    size_k = gram.shape[0]
    row = lax.broadcasted_iota(jnp.int32, gram.shape, 0)
    col = lax.broadcasted_iota(jnp.int32, gram.shape, 1)
    eye_mat = jnp.where(row == col, 1.0, 0.0)

    def whole_sum(value):
        return jnp.sum(jnp.sum(value, axis=0, keepdims=True), axis=1, keepdims=True)

    shrunk = gram + whole_sum(gram * eye_mat) / size_k * eye_mat
    scale = jnp.sqrt(whole_sum(shrunk * shrunk))
    approx = shrunk / scale
    inverse = eye_mat
    for turn in range(NS_ITERS):
        both = approx if turn == 0 else fine_dot(inverse, approx)
        factor = 0.5 * (3.0 * eye_mat - both)
        if turn == 0:
            approx, inverse = fine_dot(approx, factor), factor
        elif turn < NS_ITERS - 1:
            stacked = fine_dot(jnp.concatenate([approx, inverse], axis=0), factor)
            approx, inverse = stacked[:size_k], stacked[size_k:]
        else:
            inverse = fine_dot(inverse, factor)
    return inverse * jnp.sqrt(total / scale)


def gathered_block(gathered_ref, index):
    half = gathered_ref.shape[0] // 2
    return jnp.concatenate([gathered_ref[index], gathered_ref[half + index]], axis=0)


def newton_mixing(total, pair):
    def kernel(part_ref, other_ref, mixing_ref):
        mixing_ref[...] = newton(total, part_ref[...] + other_ref[...])

    return pl.pallas_call(
        kernel, out_shape=jax.ShapeDtypeStruct(pair[0].shape, jnp.float32), name="newton"
    )(*pair)


def newton_scores(total, pair, gathered, first_block, n_blocks):
    comps, sub = pair[0].shape[0], gathered.shape[2]

    def kernel(first_ref, part_ref, other_ref, gathered_ref, out_ref):
        mixing = newton(total, part_ref[...] + other_ref[...])
        for n in range(n_blocks):
            sums = gathered_block(gathered_ref, first_ref[0] + n)
            out_ref[pl.ds(n * sub, sub), :] = mixed_dot(mixing, sums).T

    vmem = pl.BlockSpec(memory_space=pltpu.VMEM)
    return pl.pallas_call(
        kernel,
        in_specs=[pl.BlockSpec(memory_space=pltpu.SMEM), vmem, vmem, vmem],
        out_specs=vmem,
        out_shape=jax.ShapeDtypeStruct((n_blocks * sub, comps), jnp.float32),
        name="newton_scores",
    )(first_block, *pair, gathered)


def gram_part(gathered):
    half, half_k, _ = gathered.shape
    half = half // 2

    def kernel(gathered_ref, out_ref):
        acc = None
        for n in range(half):
            sums = gathered_block(gathered_ref, n)
            add = tall_dot(sums, sums)
            acc = add if acc is None else acc + add
        out_ref[...] = acc

    return pl.pallas_call(
        kernel, out_shape=jax.ShapeDtypeStruct((2 * half_k, 2 * half_k), jnp.float32), name="gram"
    )(gathered)


def sum_and_fan(parts):
    n, half_k, sub = parts.shape

    def kernel(parts_ref, out_ref):
        acc = parts_ref[0].astype(jnp.float32)
        for i in range(1, n):
            acc = acc + parts_ref[i].astype(jnp.float32)
        acc = acc.astype(jnp.bfloat16)
        for i in range(2 * n):
            out_ref[i] = acc

    return pl.pallas_call(
        kernel, out_shape=jax.ShapeDtypeStruct((2 * n, half_k, sub), jnp.bfloat16), name="fan"
    )(parts)


def step_call(
    total, where, data, coeffs=None, grads=None, values=None, mixing=None, gathered=None, n_sub=None
):
    piece_rows, feats = data[0].shape
    n_pieces = len(data)
    pooled = n_pieces * piece_rows
    half_k = (coeffs if coeffs is not None else values).shape[0]
    low = jnp.bfloat16
    vmem, smem = pl.BlockSpec(memory_space=pltpu.VMEM), pl.BlockSpec(memory_space=pltpu.SMEM)
    args, specs, shapes = [where, *data], [smem] + [pl.BlockSpec(memory_space=pl.ANY)] * n_pieces, []
    names = []

    def give(name, *arrays):
        for i, array in enumerate(arrays):
            names.append(f"{name}{i}")
            args.append(array)
            specs.append(vmem)

    if values is None:
        give("coeffs", coeffs)
        if grads is not None:
            give("grads", *grads)
            shapes.append(("new_coeffs", jax.ShapeDtypeStruct((half_k, feats), jnp.float32)))
    else:
        give("values", values)
    if n_sub is not None:
        sub = pooled // n_sub
        shapes.append(("out_values", jax.ShapeDtypeStruct((half_k, pooled), jnp.float32)))
        shapes.append(("parts", jax.ShapeDtypeStruct((n_sub, half_k, sub), low)))
    if mixing is not None:
        give("mixing", mixing)
        give("gathered", gathered)
        shapes.append(("term", jax.ShapeDtypeStruct((half_k, feats), low)))

    def kernel(where_ref, *refs):
        pieces = refs[:n_pieces]
        at = n_pieces
        ins = dict(zip(names, refs[at : at + len(names)], strict=True))
        at += len(names)
        outs = dict(zip([name for name, _ in shapes], refs[at : at + len(shapes)], strict=True))
        held, resid, sems = refs[at + len(shapes) :]
        base, core = where_ref[0], where_ref[1]

        def copy(i):
            return pltpu.make_async_copy(
                pieces[i], held.at[pl.ds(i * piece_rows, piece_rows), :], sems.at[i]
            )

        for i in range(n_pieces):
            copy(i).start()

        def block_at(i):
            own = core if i % 2 == 0 else 1 - core
            return 2 * lax.bitwise_xor(base, i // 2) + own

        if mixing is not None:
            mixing_rows = ins["mixing0"][pl.ds(pl.multiple_of(core * half_k, half_k), half_k), :]
            sub_in = gathered.shape[2]
            ratio = piece_rows // sub_in

            def set_resid(i, value):
                sums = [
                    gathered_block(ins["gathered0"], block_at(i) * ratio + r) for r in range(ratio)
                ]
                sums = sums[0] if ratio == 1 else jnp.concatenate(sums, axis=1)
                resid[:, pl.ds(i * piece_rows, piece_rows)] = (
                    value - mixed_dot(mixing_rows, sums)
                ).astype(low)

        if values is None:
            weights = ins["coeffs0"][...]
            if grads is not None:
                grad = ins["grads0"][...].astype(jnp.float32) + ins["grads1"][...].astype(jnp.float32)
                weights = weights - step_size * (grad / total + ridge_weight * weights)
                outs["new_coeffs"][...] = weights
            weights = weights.astype(low)
            for i in range(n_pieces):
                copy(i).wait()
                value = tall_dot(weights, held[pl.ds(i * piece_rows, piece_rows), :])
                if n_sub is not None:
                    outs["out_values"][:, pl.ds(i * piece_rows, piece_rows)] = value
                    ratio_out = piece_rows // sub
                    for r in range(ratio_out):
                        outs["parts"][block_at(i) * ratio_out + r] = value[
                            :, r * sub : (r + 1) * sub
                        ].astype(low)
                if mixing is not None:
                    set_resid(i, value)
        else:
            for i in range(n_pieces):
                set_resid(i, ins["values0"][:, pl.ds(i * piece_rows, piece_rows)])
            for i in range(n_pieces):
                copy(i).wait()
        if mixing is not None:
            outs["term"][...] = jnp.dot(
                resid[...], held[...], preferred_element_type=jnp.float32
            ).astype(low)

    return pl.pallas_call(
        kernel,
        in_specs=specs,
        out_specs=[vmem] * len(shapes),
        out_shape=[shape for _, shape in shapes],
        scratch_shapes=[
            pltpu.VMEM((pooled, feats), low),
            pltpu.VMEM((half_k, pooled), low),
            pltpu.SemaphoreType.DMA((n_pieces,)),
        ],
        name="step",
    )(*args)


class Grid:
    def __init__(self, n_view, n_samp):
        self.planes, self.squares = n_view // 2, n_samp // GROUP
        self.n_samp = n_samp

    def encode(self, plane, core, square, corner):
        return (plane * 2 + core) * self.n_samp + square * GROUP + corner

    def each(self):
        for plane in range(self.planes):
            for core in range(2):
                for square in range(self.squares):
                    for corner in range(GROUP):
                        yield plane, core, square, corner

    def permute(self, value, target):
        pairs = [(self.encode(*at), self.encode(*target(*at))) for at in self.each()]
        return lax.ppermute(value, AXES, pairs)

    def swap_core(self, value):
        return self.permute(value, lambda a, c, q, p: (a, 1 - c, q, p))

    def sum_squares(self, value, wire):
        low, other = value.astype(wire), jnp.zeros(value.shape, wire)
        bit = 1
        while bit < self.squares:
            if bit > 1:
                low = (low.astype(jnp.float32) + other.astype(jnp.float32)).astype(wire)
            other = self.permute(low, lambda a, c, q, p, bit=bit: (a, c, q ^ bit, p))
            bit *= 2
        return low, other

    def sum_planes(self, value):
        bit = 1
        while bit < self.planes:
            value = value + self.permute(value, lambda a, c, q, p, bit=bit: (a ^ bit, c, q, p))
            bit *= 2
        return value


def pick(parts, index, axis=0):
    return lax.dynamic_index_in_dim(parts, index, axis, keepdims=False)


def pick(parts, index, axis=0):
    return lax.dynamic_index_in_dim(parts, index, axis, keepdims=False)


def body(view_data, init_coeffs):
    low = jnp.bfloat16
    grid = Grid(lax.axis_size("view"), lax.axis_size("samp"))
    rows, feats = view_data.shape[1:]
    comps = init_coeffs.shape[2]
    half_k, half_rows = comps // 2, rows // 2
    total = rows * lax.axis_size("samp")
    view_at, samp_at = lax.axis_index("view"), lax.axis_index("samp")
    core = view_at % 2
    square, corner = samp_at // GROUP, samp_at % GROUP
    base = 2 * core + corner % 2
    where = jnp.stack([base, core]).astype(jnp.int32)
    n_sub = GROUP * grid.planes
    sub = rows // grid.planes

    slots = [None] * GROUP

    def pool(k):
        m = corner ^ k
        piece = lax.dynamic_slice(
            view_data, (m % 2, (m // 2) * half_rows, 0), (1, half_rows, feats)
        )[0]
        slots[k] = grid.permute(
            piece, lambda a, c, q, p, k=k: (a, (p ^ k) // 2, q, 2 * c + (p ^ k) % 2)
        )

    pool(1)
    pool(0)

    coeffs_low = init_coeffs.astype(low)
    part = jnp.zeros((comps, rows), jnp.float32)
    for member in range(view_data.shape[0]):
        part = part + lax.dot_general(
            coeffs_low[member],
            view_data[member],
            (((0,), (1,)), ((), ())),
            preferred_element_type=jnp.float32,
        )
    pool(3)
    pool(2)
    mine = lax.dynamic_slice_in_dim(part, core * half_rows, half_rows, 1)
    theirs = lax.dynamic_slice_in_dim(part, (1 - core) * half_rows, half_rows, 1)
    mine = mine + grid.swap_core(theirs)
    mine, init_later = lax.optimization_barrier((mine, init_coeffs))
    mine = grid.sum_planes(mine)
    square_groups = [
        [grid.encode(a, c, q, p) for p in range(GROUP) for c in range(2)]
        for a in range(grid.planes)
        for q in range(grid.squares)
    ]
    gathered = lax.all_to_all(
        jnp.broadcast_to(mine.astype(low), (2 * GROUP, comps, half_rows)),
        AXES, 0, 0, axis_index_groups=square_groups,
    )
    local = jnp.transpose(pick(init_later, corner % 2)).reshape(2, half_k, feats)
    from_core = grid.swap_core(pick(local, 1 - core))
    coeffs = jnp.where(core == corner // 2, pick(local, core), from_core)
    gathered, coeffs = lax.optimization_barrier((gathered, coeffs))
    gathered = jnp.transpose(
        gathered.reshape(2 * GROUP, 2, half_k, half_rows // sub, sub), (1, 0, 3, 2, 4)
    ).reshape(2 * n_sub, half_k, sub)

    data = []
    for k in range(GROUP):
        data += [slots[k], grid.swap_core(slots[k ^ 2])]

    def gram_pair(gathered):
        return grid.sum_squares(gram_part(gathered), jnp.float32)

    pair = gram_pair(gathered)
    mixing = newton_mixing(total, pair)

    reduce_groups = [
        [grid.encode(a, c, q, p) for p in range(GROUP) for a in range(grid.planes)]
        for c in range(2)
        for q in range(grid.squares)
    ]
    gather_groups = [
        [
            grid.encode(a, c, q, p)
            for c in range(2)
            for p in range(GROUP)
            for a in range(grid.planes)
        ]
        for q in range(grid.squares)
    ]
    values = grads = None
    for outer_step in range(OUTER):
        for inner_step in range(INNER):
            given = {"mixing": mixing, "gathered": gathered}
            if inner_step == 0 and outer_step > 0:
                (term,) = step_call(total, where, data, values=values, **given)
            elif grads is None:
                (term,) = step_call(total, where, data, coeffs=coeffs, **given)
            else:
                coeffs, term = step_call(total, where, data, coeffs=coeffs, grads=grads, **given)
            grads = grid.sum_squares(term, low)
        coeffs, values, parts = step_call(
            total, where, data, coeffs=coeffs, grads=grads, n_sub=n_sub
        )
        grads = None
        parts = lax.all_to_all(parts, AXES, 0, 0, axis_index_groups=reduce_groups)
        gathered = lax.all_to_all(
            sum_and_fan(parts), AXES, 0, 0, axis_index_groups=gather_groups
        )
        if outer_step < OUTER - 1:
            mixing = newton_mixing(total, gram_pair(gathered))
    gathered, coeffs = lax.optimization_barrier((gathered, coeffs))
    first_block = (corner * grid.planes).astype(jnp.int32).reshape(1)
    shared = newton_scores(total, gram_pair(gathered), gathered, first_block, grid.planes)

    out_rows = feats // lax.axis_size("samp")
    pieces = []
    for k in range(GROUP):
        start = (square * GROUP + (base ^ k)) * out_rows
        piece = lax.dynamic_slice_in_dim(coeffs, start, out_rows, 1)
        pieces.append(
            grid.permute(
                piece,
                lambda a, c, q, p, k=k: (a, p // 2, q, (2 * c + p % 2) ^ k),
            )
        )
    pieces = jnp.stack(pieces)
    ordered = [pick(pieces, corner ^ r) for r in range(GROUP)]
    final = jnp.stack(
        [jnp.concatenate([ordered[member], ordered[2 + member]], axis=0).T for member in range(2)]
    )
    return (shared, final)


def solution(mesh):
    in_specs = (P("view", "samp", None), P("view", None, None))
    out_specs = (P("samp", None), P("view", "samp", None))

    return jax.shard_map(body, mesh=mesh, in_specs=in_specs, out_specs=out_specs, check_vma=False)
```

```python
import jax
import jax.numpy as jnp
from jax import lax
from jax.experimental import pallas as pl
from jax.experimental.pallas import tpu as pltpu
from jax.sharding import PartitionSpec as P


OUTER = 2
INNER = 2
NS_ITERS = 12

ridge_weight = 0.1
step_size = 0.5
AXES = ("view", "samp")
GROUP = 4

SMALL = pltpu.CompilerParams(vmem_limit_bytes=4 << 20)
LARGE = pltpu.CompilerParams(vmem_limit_bytes=16 << 20)


def split(value):
    top = value.astype(jnp.bfloat16)
    return top, (value - top.astype(jnp.float32)).astype(jnp.bfloat16)


def fine_dot(left, right):
    left_top, left_rest = split(left)
    right_top, right_rest = split(right)
    out = jnp.dot(left_top, right_rest, preferred_element_type=jnp.float32)
    out = out + jnp.dot(left_rest, right_top, preferred_element_type=jnp.float32)
    return out + jnp.dot(left_top, right_top, preferred_element_type=jnp.float32)


def tall_dot(left, right):
    return lax.dot_general(left, right, (((1,), (1,)), ((), ())), preferred_element_type=jnp.float32)


def mixed_dot(mixing, sums):
    top, rest = split(mixing)
    return jnp.dot(rest, sums, preferred_element_type=jnp.float32) + jnp.dot(
        top, sums, preferred_element_type=jnp.float32
    )


def newton(total, gram):
    size_k = gram.shape[0]
    row = lax.broadcasted_iota(jnp.int32, gram.shape, 0)
    col = lax.broadcasted_iota(jnp.int32, gram.shape, 1)
    eye_mat = jnp.where(row == col, 1.0, 0.0)

    def whole_sum(value):
        return jnp.sum(jnp.sum(value, axis=0, keepdims=True), axis=1, keepdims=True)

    shrunk = gram + whole_sum(gram * eye_mat) / size_k * eye_mat
    scale = jnp.sqrt(whole_sum(shrunk * shrunk))
    approx = shrunk / scale
    inverse = eye_mat
    for turn in range(NS_ITERS):
        both = approx if turn == 0 else fine_dot(inverse, approx)
        factor = 0.5 * (3.0 * eye_mat - both)
        if turn == 0:
            approx, inverse = fine_dot(approx, factor), factor
        elif turn < NS_ITERS - 1:
            stacked = fine_dot(jnp.concatenate([approx, inverse], axis=0), factor)
            approx, inverse = stacked[:size_k], stacked[size_k:]
        else:
            inverse = fine_dot(inverse, factor)
    return inverse * jnp.sqrt(total / scale)


def gathered_block(gathered_ref, index):
    half = gathered_ref.shape[0] // 2
    return jnp.concatenate([gathered_ref[index], gathered_ref[half + index]], axis=0)


def newton_mixing(total, pair):
    def kernel(part_ref, other_ref, mixing_ref):
        mixing_ref[...] = newton(total, part_ref[...] + other_ref[...])

    return pl.pallas_call(
        kernel, out_shape=jax.ShapeDtypeStruct(pair[0].shape, jnp.float32), name="newton", compiler_params=SMALL
    )(*pair)


def newton_scores(total, pair, gathered, where, n_blocks):
    comps, sub = pair[0].shape[0], gathered.shape[2]

    def kernel(where_ref, part_ref, other_ref, gathered_ref, out_ref):
        mixing = newton(total, part_ref[...] + other_ref[...])
        for n in range(n_blocks):
            sums = gathered_block(gathered_ref, where_ref[2] + n)
            out_ref[pl.ds(n * sub, sub), :] = mixed_dot(mixing, sums).T

    vmem = pl.BlockSpec(memory_space=pltpu.VMEM)
    return pl.pallas_call(
        kernel,
        in_specs=[pl.BlockSpec(memory_space=pltpu.SMEM), vmem, vmem, vmem],
        out_specs=vmem,
        out_shape=jax.ShapeDtypeStruct((n_blocks * sub, comps), jnp.float32),
        name="newton_scores",
        compiler_params=SMALL,
    )(where, *pair, gathered)


def gram_part(gathered):
    half, half_k, _ = gathered.shape
    half = half // 2

    def kernel(gathered_ref, out_ref):
        acc = None
        for n in range(half):
            sums = gathered_block(gathered_ref, n)
            add = tall_dot(sums, sums)
            acc = add if acc is None else acc + add
        out_ref[...] = acc

    return pl.pallas_call(
        kernel, out_shape=jax.ShapeDtypeStruct((2 * half_k, 2 * half_k), jnp.float32), name="gram", compiler_params=SMALL
    )(gathered)


def sum_and_fan(parts):
    n, half_k, sub = parts.shape

    def kernel(parts_ref, out_ref):
        acc = parts_ref[0].astype(jnp.float32)
        for i in range(1, n):
            acc = acc + parts_ref[i].astype(jnp.float32)
        acc = acc.astype(jnp.bfloat16)
        for i in range(2 * n):
            out_ref[i] = acc

    return pl.pallas_call(
        kernel, out_shape=jax.ShapeDtypeStruct((2 * n, half_k, sub), jnp.bfloat16), name="fan", compiler_params=SMALL
    )(parts)


def step_call(
    total, where, data, coeffs=None, grads=None, values=None, mixing=None, gathered=None, n_sub=None
):
    piece_rows, feats = data[0].shape
    n_pieces = len(data)
    pooled = n_pieces * piece_rows
    half_k = (coeffs if coeffs is not None else values).shape[0]
    low = jnp.bfloat16
    vmem, smem = pl.BlockSpec(memory_space=pltpu.VMEM), pl.BlockSpec(memory_space=pltpu.SMEM)
    args, specs, shapes = [where, *data], [smem] + [vmem] * n_pieces, []
    names = []

    def give(name, *arrays):
        for i, array in enumerate(arrays):
            names.append(f"{name}{i}")
            args.append(array)
            specs.append(vmem)

    if values is None:
        give("coeffs", coeffs)
        if grads is not None:
            give("grads", *grads)
            shapes.append(("new_coeffs", jax.ShapeDtypeStruct((half_k, feats), jnp.float32)))
    else:
        give("values", values)
    if n_sub is not None:
        sub = pooled // n_sub
        shapes.append(("out_values", jax.ShapeDtypeStruct((half_k, pooled), jnp.float32)))
        shapes.append(("parts", jax.ShapeDtypeStruct((n_sub, half_k, sub), low)))
    if mixing is not None:
        give("mixing", mixing)
        give("gathered", gathered)
        shapes.append(("term", jax.ShapeDtypeStruct((half_k, feats), low)))

    def kernel(where_ref, *refs):
        pieces = refs[:n_pieces]
        at = n_pieces
        ins = dict(zip(names, refs[at : at + len(names)], strict=True))
        at += len(names)
        outs = dict(zip([name for name, _ in shapes], refs[at : at + len(shapes)], strict=True))
        (resid,) = refs[at + len(shapes) :]
        base, core = where_ref[0], where_ref[1]

        def block_at(i):
            own = core if i % 2 == 0 else 1 - core
            return 2 * lax.bitwise_xor(base, i // 2) + own

        if mixing is not None:
            mixing_rows = ins["mixing0"][pl.ds(pl.multiple_of(core * half_k, half_k), half_k), :]
            sub_in = gathered.shape[2]
            ratio = piece_rows // sub_in

            def set_resid(i, value):
                sums = [
                    gathered_block(ins["gathered0"], block_at(i) * ratio + r) for r in range(ratio)
                ]
                sums = sums[0] if ratio == 1 else jnp.concatenate(sums, axis=1)
                resid[:, pl.ds(i * piece_rows, piece_rows)] = (
                    value - mixed_dot(mixing_rows, sums)
                ).astype(low)

        if values is None:
            weights = ins["coeffs0"][...]
            if grads is not None:
                grad = ins["grads0"][...].astype(jnp.float32) + ins["grads1"][...].astype(jnp.float32)
                weights = weights - step_size * (grad / total + ridge_weight * weights)
                outs["new_coeffs"][...] = weights
            weights = weights.astype(low)
            for i in range(n_pieces):
                value = tall_dot(weights, pieces[i][...])
                if n_sub is not None:
                    outs["out_values"][:, pl.ds(i * piece_rows, piece_rows)] = value
                    ratio_out = piece_rows // sub
                    for r in range(ratio_out):
                        outs["parts"][block_at(i) * ratio_out + r] = value[
                            :, r * sub : (r + 1) * sub
                        ].astype(low)
                if mixing is not None:
                    set_resid(i, value)
        else:
            for i in range(n_pieces):
                set_resid(i, ins["values0"][:, pl.ds(i * piece_rows, piece_rows)])
        if mixing is not None:
            wide = feats // 4
            for n in range(4):
                acc = None
                for i in range(n_pieces):
                    add = jnp.dot(
                        resid[:, pl.ds(i * piece_rows, piece_rows)],
                        pieces[i][:, pl.ds(n * wide, wide)],
                        preferred_element_type=jnp.float32,
                    )
                    acc = add if acc is None else acc + add
                outs["term"][:, pl.ds(n * wide, wide)] = acc.astype(low)

    return pl.pallas_call(
        kernel,
        in_specs=specs,
        out_specs=[vmem] * len(shapes),
        out_shape=[shape for _, shape in shapes],
        scratch_shapes=[
            pltpu.VMEM((half_k, pooled), low),
        ],
        name="step",
        compiler_params=LARGE,
    )(*args)


class Grid:
    def __init__(self, n_view, n_samp):
        self.planes, self.squares = n_view // 2, n_samp // GROUP
        self.n_samp = n_samp

    def encode(self, plane, core, square, corner):
        return (plane * 2 + core) * self.n_samp + square * GROUP + corner

    def each(self):
        for plane in range(self.planes):
            for core in range(2):
                for square in range(self.squares):
                    for corner in range(GROUP):
                        yield plane, core, square, corner

    def permute(self, value, target):
        pairs = [(self.encode(*at), self.encode(*target(*at))) for at in self.each()]
        return lax.ppermute(value, AXES, pairs)

    def swap_core(self, value):
        return self.permute(value, lambda a, c, q, p: (a, 1 - c, q, p))

    def sum_squares(self, value, wire):
        low, other = value.astype(wire), jnp.zeros(value.shape, wire)
        bit = 1
        while bit < self.squares:
            if bit > 1:
                low = (low.astype(jnp.float32) + other.astype(jnp.float32)).astype(wire)
            other = self.permute(low, lambda a, c, q, p, bit=bit: (a, c, q ^ bit, p))
            bit *= 2
        return low, other

    def sum_planes(self, value):
        bit = 1
        while bit < self.planes:
            value = value + self.permute(value, lambda a, c, q, p, bit=bit: (a ^ bit, c, q, p))
            bit *= 2
        return value


def pick(parts, index):
    return lax.dynamic_index_in_dim(parts, index, 0, keepdims=False, allow_negative_indices=False)


def cut(value, start, size, axis):
    return lax.dynamic_slice_in_dim(value, start, size, axis, allow_negative_indices=False)


def pick(parts, index):
    return lax.dynamic_index_in_dim(parts, index, 0, keepdims=False, allow_negative_indices=False)


def cut(value, start, size, axis):
    return lax.dynamic_slice_in_dim(value, start, size, axis, allow_negative_indices=False)


def body(view_data, init_coeffs):
    low = jnp.bfloat16
    grid = Grid(lax.axis_size("view"), lax.axis_size("samp"))
    rows, feats = view_data.shape[1:]
    comps = init_coeffs.shape[2]
    half_k, half_rows = comps // 2, rows // 2
    total = rows * lax.axis_size("samp")
    n_sub = GROUP * grid.planes
    sub = rows // grid.planes
    out_rows = feats // lax.axis_size("samp")
    view_at = lax.axis_index("view").astype(jnp.uint32)
    samp_at = lax.axis_index("samp").astype(jnp.uint32)
    core, other_core = view_at & 1, 1 - (view_at & 1)
    corner = samp_at & (GROUP - 1)
    base = 2 * core + (corner & 1)
    own_view = corner & 1
    holder = core == (corner >> 1)
    where = jnp.stack([base, core, corner * grid.planes]).astype(jnp.int32)
    pool_at = [((corner ^ k) & 1, ((corner ^ k) >> 1) * half_rows) for k in range(GROUP)]
    own_at, their_at = core * half_rows, other_core * half_rows
    out_at = [((samp_at & ~jnp.uint32(GROUP - 1)) + (base ^ k)) * out_rows for k in range(GROUP)]
    order_at = [corner ^ r for r in range(GROUP)]
    zero = jnp.uint32(0)
    held = (core, other_core, own_view, holder, where, pool_at, own_at, their_at, out_at, order_at)
    view_data, init_coeffs, held = lax.optimization_barrier((view_data, init_coeffs, held))
    core, other_core, own_view, holder, where, pool_at, own_at, their_at, out_at, order_at = held

    slots = [None] * GROUP

    def pool(k):
        at = (*pool_at[k], zero)
        piece = lax.dynamic_slice(
            view_data, at, (1, half_rows, feats), allow_negative_indices=False
        )[0]
        slots[k] = grid.permute(
            piece, lambda a, c, q, p, k=k: (a, (p ^ k) // 2, q, 2 * c + (p ^ k) % 2)
        )

    pool(1)
    pool(0)

    coeffs_low = init_coeffs.astype(low)
    part = jnp.zeros((comps, rows), jnp.float32)
    for member in range(view_data.shape[0]):
        part = part + lax.dot_general(
            coeffs_low[member],
            view_data[member],
            (((0,), (1,)), ((), ())),
            preferred_element_type=jnp.float32,
        )
    pool(3)
    pool(2)
    mine = cut(part, own_at, half_rows, 1)
    theirs = cut(part, their_at, half_rows, 1)
    mine = mine + grid.swap_core(theirs)
    mine, init_later = lax.optimization_barrier((mine, init_coeffs))
    mine = grid.sum_planes(mine)
    square_groups = [
        [grid.encode(a, c, q, p) for p in range(GROUP) for c in range(2)]
        for a in range(grid.planes)
        for q in range(grid.squares)
    ]
    gathered = lax.all_to_all(
        jnp.broadcast_to(mine.astype(low), (2 * GROUP, comps, half_rows)),
        AXES, 0, 0, axis_index_groups=square_groups,
    )
    local = jnp.transpose(pick(init_later, own_view)).reshape(2, half_k, feats)
    from_core = grid.swap_core(pick(local, other_core))
    coeffs = jnp.where(holder, pick(local, core), from_core)
    gathered, coeffs = lax.optimization_barrier((gathered, coeffs))
    gathered = jnp.transpose(
        gathered.reshape(2 * GROUP, 2, half_k, half_rows // sub, sub), (1, 0, 3, 2, 4)
    ).reshape(2 * n_sub, half_k, sub)

    data = []
    for k in range(GROUP):
        data += [slots[k], grid.swap_core(slots[k ^ 2])]

    def gram_pair(gathered):
        return grid.sum_squares(gram_part(gathered), jnp.float32)

    pair = gram_pair(gathered)
    mixing = newton_mixing(total, pair)

    reduce_groups = [
        [grid.encode(a, c, q, p) for p in range(GROUP) for a in range(grid.planes)]
        for c in range(2)
        for q in range(grid.squares)
    ]
    gather_groups = [
        [
            grid.encode(a, c, q, p)
            for c in range(2)
            for p in range(GROUP)
            for a in range(grid.planes)
        ]
        for q in range(grid.squares)
    ]
    values = grads = None
    for outer_step in range(OUTER):
        for inner_step in range(INNER):
            given = {"mixing": mixing, "gathered": gathered}
            if inner_step == 0 and outer_step > 0:
                (term,) = step_call(total, where, data, values=values, **given)
            elif grads is None:
                (term,) = step_call(total, where, data, coeffs=coeffs, **given)
            else:
                coeffs, term = step_call(total, where, data, coeffs=coeffs, grads=grads, **given)
            grads = grid.sum_squares(term, low)
        coeffs, values, parts = step_call(
            total, where, data, coeffs=coeffs, grads=grads, n_sub=n_sub
        )
        grads = None
        parts = lax.all_to_all(parts, AXES, 0, 0, axis_index_groups=reduce_groups)
        gathered = lax.all_to_all(
            sum_and_fan(parts), AXES, 0, 0, axis_index_groups=gather_groups
        )
        if outer_step < OUTER - 1:
            mixing = newton_mixing(total, gram_pair(gathered))
    gathered, coeffs = lax.optimization_barrier((gathered, coeffs))
    shared = newton_scores(total, gram_pair(gathered), gathered, where, grid.planes)

    pieces = []
    for k in range(GROUP):
        piece = cut(coeffs, out_at[k], out_rows, 1)
        pieces.append(
            grid.permute(
                piece,
                lambda a, c, q, p, k=k: (a, p // 2, q, (2 * c + p % 2) ^ k),
            )
        )
    pieces = jnp.stack(pieces)
    ordered = [pick(pieces, order_at[r]) for r in range(GROUP)]
    final = jnp.stack(
        [jnp.concatenate([ordered[member], ordered[2 + member]], axis=0).T for member in range(2)]
    )
    return (shared, final)


def solution(mesh):
    in_specs = (P("view", "samp", None), P("view", None, None))
    out_specs = (P("samp", None), P("view", "samp", None))

    return jax.shard_map(body, mesh=mesh, in_specs=in_specs, out_specs=out_specs, check_vma=False)
```

```python
import jax
import jax.numpy as jnp
from jax import lax
from jax.experimental import pallas as pl
from jax.experimental.pallas import tpu as pltpu
from jax.sharding import PartitionSpec as P


OUTER = 2
INNER = 2
NS_ITERS = 12

ridge_weight = 0.1
step_size = 0.5
AXES = ("view", "samp")
GROUP = 4

SMALL = pltpu.CompilerParams(vmem_limit_bytes=4 << 20)
LARGE = pltpu.CompilerParams(vmem_limit_bytes=16 << 20)


def split(value):
    top = value.astype(jnp.bfloat16)
    return top, (value - top.astype(jnp.float32)).astype(jnp.bfloat16)


def fine_dot(left, right):
    left_top, left_rest = split(left)
    right_top, right_rest = split(right)
    out = jnp.dot(left_top, right_rest, preferred_element_type=jnp.float32)
    out = out + jnp.dot(left_rest, right_top, preferred_element_type=jnp.float32)
    return out + jnp.dot(left_top, right_top, preferred_element_type=jnp.float32)


def tall_dot(left, right):
    return lax.dot_general(left, right, (((1,), (1,)), ((), ())), preferred_element_type=jnp.float32)


def mixed_dot(mixing, sums):
    top, rest = split(mixing)
    return jnp.dot(rest, sums, preferred_element_type=jnp.float32) + jnp.dot(
        top, sums, preferred_element_type=jnp.float32
    )


def newton(total, gram):
    size_k = gram.shape[0]
    row = lax.broadcasted_iota(jnp.int32, gram.shape, 0)
    col = lax.broadcasted_iota(jnp.int32, gram.shape, 1)
    eye_mat = jnp.where(row == col, 1.0, 0.0)

    def whole_sum(value):
        return jnp.sum(jnp.sum(value, axis=0, keepdims=True), axis=1, keepdims=True)

    shrunk = gram + whole_sum(gram * eye_mat) / size_k * eye_mat
    scale = jnp.sqrt(whole_sum(shrunk * shrunk))
    approx = shrunk / scale
    inverse = eye_mat
    for turn in range(NS_ITERS):
        both = approx if turn == 0 else fine_dot(inverse, approx)
        factor = 0.5 * (3.0 * eye_mat - both)
        if turn == 0:
            approx, inverse = fine_dot(approx, factor), factor
        elif turn < NS_ITERS - 1:
            stacked = fine_dot(jnp.concatenate([approx, inverse], axis=0), factor)
            approx, inverse = stacked[:size_k], stacked[size_k:]
        else:
            inverse = fine_dot(inverse, factor)
    return inverse * jnp.sqrt(total / scale)


def gathered_block(gathered_ref, index, comps):
    if gathered_ref.shape[1] == comps:
        return gathered_ref[index]
    half = gathered_ref.shape[0] // 2
    return jnp.concatenate([gathered_ref[index], gathered_ref[half + index]], axis=0)


def newton_mixing(total, pair):
    def kernel(part_ref, other_ref, mixing_ref):
        mixing_ref[...] = newton(total, part_ref[...] + other_ref[...])

    return pl.pallas_call(
        kernel, out_shape=jax.ShapeDtypeStruct(pair[0].shape, jnp.float32), name="newton", compiler_params=SMALL
    )(*pair)


def newton_scores(total, pair, gathered, where, n_blocks):
    comps, sub = pair[0].shape[0], gathered.shape[2]

    def kernel(where_ref, part_ref, other_ref, gathered_ref, out_ref):
        mixing = newton(total, part_ref[...] + other_ref[...])
        for n in range(n_blocks):
            sums = gathered_block(gathered_ref, where_ref[2] + n, comps)
            out_ref[pl.ds(n * sub, sub), :] = mixed_dot(mixing, sums).T

    vmem = pl.BlockSpec(memory_space=pltpu.VMEM)
    return pl.pallas_call(
        kernel,
        in_specs=[pl.BlockSpec(memory_space=pltpu.SMEM), vmem, vmem, vmem],
        out_specs=vmem,
        out_shape=jax.ShapeDtypeStruct((n_blocks * sub, comps), jnp.float32),
        name="newton_scores",
        compiler_params=SMALL,
    )(where, *pair, gathered)


def gram_part(gathered, comps):
    count = gathered.shape[0] * gathered.shape[1] // comps

    def kernel(gathered_ref, out_ref):
        acc = None
        for n in range(count):
            sums = gathered_block(gathered_ref, n, comps)
            add = tall_dot(sums, sums)
            acc = add if acc is None else acc + add
        out_ref[...] = acc

    return pl.pallas_call(
        kernel,
        out_shape=jax.ShapeDtypeStruct((comps, comps), jnp.float32),
        name="gram",
        compiler_params=SMALL,
    )(gathered)


def first_coeffs(init_coeffs, where):
    _, feats, comps = init_coeffs.shape
    half_k = comps // 2

    def kernel(where_ref, init_ref, own_ref, other_ref):
        turned = init_ref[where_ref[3]].T
        first, second = turned[:half_k], turned[half_k:]
        swap = where_ref[1] == 1
        own_ref[...] = jnp.where(swap, second, first)
        other_ref[...] = jnp.where(swap, first, second)

    vmem = pl.BlockSpec(memory_space=pltpu.VMEM)
    half = jax.ShapeDtypeStruct((half_k, feats), jnp.float32)
    return pl.pallas_call(
        kernel,
        in_specs=[pl.BlockSpec(memory_space=pltpu.SMEM), vmem],
        out_specs=[vmem, vmem],
        out_shape=[half, half],
        name="first_coeffs",
        compiler_params=LARGE,
    )(where, init_coeffs)


def sum_and_fan(parts):
    n, half_k, sub = parts.shape

    def kernel(parts_ref, out_ref):
        acc = parts_ref[0].astype(jnp.float32)
        for i in range(1, n):
            acc = acc + parts_ref[i].astype(jnp.float32)
        acc = acc.astype(jnp.bfloat16)
        for i in range(2 * n):
            out_ref[i] = acc

    return pl.pallas_call(
        kernel, out_shape=jax.ShapeDtypeStruct((2 * n, half_k, sub), jnp.bfloat16), name="fan", compiler_params=SMALL
    )(parts)


def step_call(
    total,
    where,
    data,
    coeffs=None,
    grads=None,
    values=None,
    mixing=None,
    gathered=None,
    n_sub=None,
):
    piece_rows, feats = data[0].shape
    n_pieces = len(data)
    pooled = n_pieces * piece_rows
    half_k = (coeffs if coeffs is not None else values).shape[0]
    low = jnp.bfloat16
    vmem, smem = pl.BlockSpec(memory_space=pltpu.VMEM), pl.BlockSpec(memory_space=pltpu.SMEM)
    args, specs, shapes = [where, *data], [smem] + [vmem] * n_pieces, []
    names = []

    def give(name, *arrays):
        for i, array in enumerate(arrays):
            names.append(f"{name}{i}")
            args.append(array)
            specs.append(vmem)

    if values is None:
        give("coeffs", coeffs)
        if grads is not None:
            give("grads", *grads)
            shapes.append(("new_coeffs", jax.ShapeDtypeStruct((half_k, feats), jnp.float32)))
    else:
        give("values", values)
    if n_sub is not None:
        sub = pooled // n_sub
        shapes.append(("out_values", jax.ShapeDtypeStruct((half_k, pooled), jnp.float32)))
        shapes.append(("parts", jax.ShapeDtypeStruct((n_sub, half_k, sub), low)))
    if mixing is not None:
        give("mixing", mixing)
        give("gathered", gathered)
        shapes.append(("term", jax.ShapeDtypeStruct((half_k, feats), low)))

    def kernel(where_ref, *refs):
        pieces = refs[:n_pieces]
        at = n_pieces
        ins = dict(zip(names, refs[at : at + len(names)], strict=True))
        at += len(names)
        outs = dict(zip([name for name, _ in shapes], refs[at : at + len(shapes)], strict=True))
        (resid,) = refs[at + len(shapes) :]
        base, core = where_ref[0], where_ref[1]

        def block_at(i):
            own = core if i % 2 == 0 else 1 - core
            return 2 * lax.bitwise_xor(base, i // 2) + own

        if mixing is not None:
            mixing_rows = ins["mixing0"][pl.ds(pl.multiple_of(core * half_k, half_k), half_k), :]
            sub_in = gathered.shape[2]
            ratio = piece_rows // sub_in

            def set_resid(i, value):
                sums = [
                    gathered_block(ins["gathered0"], block_at(i) * ratio + r, 2 * half_k)
                    for r in range(ratio)
                ]
                sums = sums[0] if ratio == 1 else jnp.concatenate(sums, axis=1)
                resid[:, pl.ds(i * piece_rows, piece_rows)] = (
                    value - mixed_dot(mixing_rows, sums)
                ).astype(low)

        if values is None:
            weights = ins["coeffs0"][...]
            if grads is not None:
                grad = ins["grads0"][...].astype(jnp.float32) + ins["grads1"][...].astype(jnp.float32)
                weights = weights - step_size * (grad / total + ridge_weight * weights)
                outs["new_coeffs"][...] = weights
            weights = weights.astype(low)
            for i in range(n_pieces):
                value = tall_dot(weights, pieces[i][...])
                if n_sub is not None:
                    outs["out_values"][:, pl.ds(i * piece_rows, piece_rows)] = value
                    ratio_out = piece_rows // sub
                    for r in range(ratio_out):
                        outs["parts"][block_at(i) * ratio_out + r] = value[
                            :, r * sub : (r + 1) * sub
                        ].astype(low)
                if mixing is not None:
                    set_resid(i, value)
        else:
            for i in range(n_pieces):
                set_resid(i, ins["values0"][:, pl.ds(i * piece_rows, piece_rows)])
        if mixing is not None:
            wide = feats // 4
            for n in range(4):
                acc = None
                for i in range(n_pieces):
                    add = jnp.dot(
                        resid[:, pl.ds(i * piece_rows, piece_rows)],
                        pieces[i][:, pl.ds(n * wide, wide)],
                        preferred_element_type=jnp.float32,
                    )
                    acc = add if acc is None else acc + add
                outs["term"][:, pl.ds(n * wide, wide)] = acc.astype(low)

    return pl.pallas_call(
        kernel,
        in_specs=specs,
        out_specs=[vmem] * len(shapes),
        out_shape=[shape for _, shape in shapes],
        scratch_shapes=[
            pltpu.VMEM((half_k, pooled), low),
        ],
        name="step",
        compiler_params=LARGE,
    )(*args)


class Grid:
    def __init__(self, n_view, n_samp):
        self.planes, self.squares = n_view // 2, n_samp // GROUP
        self.n_samp = n_samp

    def encode(self, plane, core, square, corner):
        return (plane * 2 + core) * self.n_samp + square * GROUP + corner

    def each(self):
        for plane in range(self.planes):
            for core in range(2):
                for square in range(self.squares):
                    for corner in range(GROUP):
                        yield plane, core, square, corner

    def permute(self, value, target):
        pairs = [(self.encode(*at), self.encode(*target(*at))) for at in self.each()]
        return lax.ppermute(value, AXES, pairs)

    def swap_core(self, value):
        return self.permute(value, lambda a, c, q, p: (a, 1 - c, q, p))

    def sum_squares(self, value, wire):
        low, other = value.astype(wire), jnp.zeros(value.shape, wire)
        bit = 1
        while bit < self.squares:
            if bit > 1:
                low = (low.astype(jnp.float32) + other.astype(jnp.float32)).astype(wire)
            other = self.permute(low, lambda a, c, q, p, bit=bit: (a, c, q ^ bit, p))
            bit *= 2
        return low, other

    def sum_planes(self, value):
        bit = 1
        while bit < self.planes:
            value = value + self.permute(value, lambda a, c, q, p, bit=bit: (a ^ bit, c, q, p))
            bit *= 2
        return value


def pick(parts, index):
    return lax.dynamic_index_in_dim(parts, index, 0, keepdims=False, allow_negative_indices=False)


def cut(value, start, size, axis):
    return lax.dynamic_slice_in_dim(value, start, size, axis, allow_negative_indices=False)


def pick(parts, index):
    return lax.dynamic_index_in_dim(parts, index, 0, keepdims=False, allow_negative_indices=False)


def cut(value, start, size, axis):
    return lax.dynamic_slice_in_dim(value, start, size, axis, allow_negative_indices=False)


def body(view_data, init_coeffs):
    low = jnp.bfloat16
    grid = Grid(lax.axis_size("view"), lax.axis_size("samp"))
    rows, feats = view_data.shape[1:]
    comps = init_coeffs.shape[2]
    half_rows = rows // 2
    total = rows * lax.axis_size("samp")
    n_sub = GROUP * grid.planes
    out_rows = feats // lax.axis_size("samp")
    view_at = lax.axis_index("view").astype(jnp.uint32)
    samp_at = lax.axis_index("samp").astype(jnp.uint32)
    core, other_core = view_at & 1, 1 - (view_at & 1)
    corner = samp_at & (GROUP - 1)
    base = 2 * core + (corner & 1)
    holder = (core == (corner >> 1)).astype(jnp.uint32)
    where = jnp.stack([base, core, corner * grid.planes, corner & 1]).astype(jnp.int32)
    pool_at = [((corner ^ k) & 1, ((corner ^ k) >> 1) * half_rows) for k in range(GROUP)]
    own_at, their_at = core * half_rows, other_core * half_rows
    out_at = [((samp_at & ~jnp.uint32(GROUP - 1)) + (base ^ k)) * out_rows for k in range(GROUP)]
    order_at = [corner ^ r for r in range(GROUP)]
    zero = jnp.uint32(0)
    held = (where, holder, pool_at, own_at, their_at, out_at, order_at)
    view_data, init_coeffs, held = lax.optimization_barrier((view_data, init_coeffs, held))
    where, holder, pool_at, own_at, their_at, out_at, order_at = held

    slots = [None] * GROUP

    def slice_piece(source, k):
        at = (*pool_at[k], zero)
        return lax.dynamic_slice(source, at, (1, half_rows, feats), allow_negative_indices=False)[0]

    early = [slice_piece(view_data, 1), slice_piece(view_data, 0)]
    view_later, *early = lax.optimization_barrier((view_data, *early))
    late = [slice_piece(view_later, 3), slice_piece(view_later, 2)]
    cut_pieces = {1: early[0], 0: early[1], 3: late[0], 2: late[1]}

    def pool(k):
        piece = cut_pieces[k]
        slots[k] = grid.permute(
            piece, lambda a, c, q, p, k=k: (a, (p ^ k) // 2, q, 2 * c + (p ^ k) % 2)
        )

    pool(1)
    pool(0)

    coeffs_low = init_coeffs.astype(low)
    part = jnp.zeros((comps, rows), jnp.float32)
    for member in range(view_data.shape[0]):
        part = part + lax.dot_general(
            coeffs_low[member],
            view_data[member],
            (((0,), (1,)), ((), ())),
            preferred_element_type=jnp.float32,
        )
    pool(3)
    pool(2)
    mine = cut(part, own_at, half_rows, 1)
    theirs = cut(part, their_at, half_rows, 1)
    mine = mine + grid.swap_core(theirs)
    mine = grid.sum_planes(mine)
    square_groups = [
        [grid.encode(a, c, q, p) for p in range(GROUP) for c in range(2)]
        for a in range(grid.planes)
        for q in range(grid.squares)
    ]
    gathered = lax.all_to_all(
        jnp.broadcast_to(mine.astype(low), (2 * GROUP, comps, half_rows)),
        AXES, 0, 0, axis_index_groups=square_groups,
    )
    coeffs, for_core = first_coeffs(init_coeffs, where)
    from_core = grid.swap_core(for_core)
    coeffs = jnp.where(holder == 1, coeffs, from_core)
    gathered, coeffs = lax.optimization_barrier((gathered, coeffs))

    shared_slots = {}
    for k in range(GROUP):
        shared_slots[k ^ 2] = grid.swap_core(slots[k])
    data = []
    for k in range(GROUP):
        data += [slots[k], shared_slots[k]]

    def gram_pair(gathered):
        return grid.sum_squares(gram_part(gathered, comps), jnp.float32)

    pair = gram_pair(gathered)
    mixing = newton_mixing(total, pair)

    reduce_groups = [
        [grid.encode(a, c, q, p) for p in range(GROUP) for a in range(grid.planes)]
        for c in range(2)
        for q in range(grid.squares)
    ]
    gather_groups = [
        [
            grid.encode(a, c, q, p)
            for c in range(2)
            for p in range(GROUP)
            for a in range(grid.planes)
        ]
        for q in range(grid.squares)
    ]
    values = grads = None
    for outer_step in range(OUTER):
        for inner_step in range(INNER):
            given = {"mixing": mixing, "gathered": gathered}
            if inner_step == 0 and outer_step > 0:
                (term,) = step_call(total, where, data, values=values, **given)
            elif grads is None:
                (term,) = step_call(total, where, data, coeffs=coeffs, **given)
            else:
                coeffs, term = step_call(total, where, data, coeffs=coeffs, grads=grads, **given)
            grads = grid.sum_squares(term, low)
        coeffs, values, parts = step_call(
            total, where, data, coeffs=coeffs, grads=grads, n_sub=n_sub
        )
        grads = None
        parts = lax.all_to_all(parts, AXES, 0, 0, axis_index_groups=reduce_groups)
        gathered = lax.all_to_all(sum_and_fan(parts), AXES, 0, 0, axis_index_groups=gather_groups)
        if outer_step < OUTER - 1:
            mixing = newton_mixing(total, gram_pair(gathered))
    pair = gram_pair(gathered)
    shared = newton_scores(total, pair, gathered, where, grid.planes)

    pieces = []
    for k in range(GROUP):
        piece = cut(coeffs, out_at[k], out_rows, 1)
        pieces.append(
            grid.permute(
                piece,
                lambda a, c, q, p, k=k: (a, p // 2, q, (2 * c + p % 2) ^ k),
            )
        )
    pieces = jnp.stack(pieces)
    ordered = [pick(pieces, order_at[r]) for r in range(GROUP)]
    final = jnp.stack(
        [jnp.concatenate([ordered[member], ordered[2 + member]], axis=0).T for member in range(2)]
    )
    return (shared, final)


def solution(mesh):
    in_specs = (P("view", "samp", None), P("view", None, None))
    out_specs = (P("samp", None), P("view", "samp", None))

    return jax.shard_map(body, mesh=mesh, in_specs=in_specs, out_specs=out_specs, check_vma=False)
```

```python
import jax
import jax.numpy as jnp
from jax import lax
from jax.experimental import pallas as pl
from jax.experimental.pallas import tpu as pltpu
from jax.sharding import PartitionSpec as P


OUTER = 2
INNER = 2
NS_ITERS = 12

ridge_weight = 0.1
step_size = 0.5
AXES = ("view", "samp")
SETS = 2
GROUP = 4

SMALL = pltpu.CompilerParams(vmem_limit_bytes=4 << 20)
LARGE = pltpu.CompilerParams(vmem_limit_bytes=16 << 20)


def split(value):
    top = value.astype(jnp.bfloat16)
    return top, (value - top.astype(jnp.float32)).astype(jnp.bfloat16)


def fine_dot(left, right):
    left_top, left_rest = split(left)
    right_top, right_rest = split(right)
    out = jnp.dot(left_top, right_rest, preferred_element_type=jnp.float32)
    out = out + jnp.dot(left_rest, right_top, preferred_element_type=jnp.float32)
    return out + jnp.dot(left_top, right_top, preferred_element_type=jnp.float32)


def tall_dot(left, right):
    return lax.dot_general(left, right, (((1,), (1,)), ((), ())), preferred_element_type=jnp.float32)


def mixed_dot(mixing, sums):
    top, rest = split(mixing)
    return jnp.dot(rest, sums, preferred_element_type=jnp.float32) + jnp.dot(
        top, sums, preferred_element_type=jnp.float32
    )


def newton(total, gram):
    size_k = gram.shape[0]
    row = lax.broadcasted_iota(jnp.int32, gram.shape, 0)
    col = lax.broadcasted_iota(jnp.int32, gram.shape, 1)
    eye_mat = jnp.where(row == col, 1.0, 0.0)

    def whole_sum(value):
        return jnp.sum(jnp.sum(value, axis=0, keepdims=True), axis=1, keepdims=True)

    shrunk = gram + whole_sum(gram * eye_mat) / size_k * eye_mat
    scale = jnp.sqrt(whole_sum(shrunk * shrunk))
    approx = shrunk / scale
    inverse = 0.5 * (3.0 * eye_mat - approx)
    approx = fine_dot(approx, inverse)

    def turn(_, state):
        approx, inverse = state
        factor = 0.5 * (3.0 * eye_mat - fine_dot(inverse, approx))
        stacked = fine_dot(jnp.concatenate([approx, inverse], axis=0), factor)
        return stacked[:size_k], stacked[size_k:]

    approx, inverse = lax.fori_loop(1, NS_ITERS - 1, turn, (approx, inverse))
    factor = 0.5 * (3.0 * eye_mat - fine_dot(inverse, approx))
    inverse = fine_dot(inverse, factor)
    return inverse * jnp.sqrt(total / scale)


def gathered_block(gathered_ref, index, comps):
    if gathered_ref.shape[1] == comps:
        return gathered_ref[index]
    half = gathered_ref.shape[0] // 2
    return jnp.concatenate([gathered_ref[index], gathered_ref[half + index]], axis=0)


def newton_mixing(total, pair):
    def kernel(part_ref, other_ref, mixing_ref):
        mixing_ref[...] = newton(total, part_ref[...] + other_ref[...])

    return pl.pallas_call(
        kernel, out_shape=jax.ShapeDtypeStruct(pair[0].shape, jnp.float32), name="newton", compiler_params=SMALL
    )(*pair)


def newton_scores(total, pair, gathered, where, n_blocks):
    comps, sub = pair[0].shape[0], gathered.shape[2]

    def kernel(where_ref, part_ref, other_ref, gathered_ref, out_ref):
        mixing = newton(total, part_ref[...] + other_ref[...])
        for n in range(n_blocks):
            sums = gathered_block(gathered_ref, where_ref[2] + n, comps)
            out_ref[pl.ds(n * sub, sub), :] = mixed_dot(mixing, sums).T

    vmem = pl.BlockSpec(memory_space=pltpu.VMEM)
    return pl.pallas_call(
        kernel,
        in_specs=[pl.BlockSpec(memory_space=pltpu.SMEM), vmem, vmem, vmem],
        out_specs=vmem,
        out_shape=jax.ShapeDtypeStruct((n_blocks * sub, comps), jnp.float32),
        name="newton_scores",
        compiler_params=SMALL,
    )(where, *pair, gathered)


def gram_part(gathered, comps):
    count = gathered.shape[0] * gathered.shape[1] // comps

    def kernel(gathered_ref, out_ref):
        acc = None
        for n in range(count):
            sums = gathered_block(gathered_ref, n, comps)
            add = tall_dot(sums, sums)
            acc = add if acc is None else acc + add
        out_ref[...] = acc

    return pl.pallas_call(
        kernel,
        out_shape=jax.ShapeDtypeStruct((comps, comps), jnp.float32),
        name="gram",
        compiler_params=SMALL,
    )(gathered)


def first_coeffs(init_coeffs, where):
    _, feats, comps = init_coeffs.shape
    half_k = comps // 2

    def kernel(where_ref, init_ref, own_ref, other_ref):
        turned = init_ref[where_ref[3]].T
        first, second = turned[:half_k], turned[half_k:]
        swap = where_ref[1] == 1
        own_ref[...] = jnp.where(swap, second, first)
        other_ref[...] = jnp.where(swap, first, second)

    vmem = pl.BlockSpec(memory_space=pltpu.VMEM)
    half = jax.ShapeDtypeStruct((half_k, feats), jnp.float32)
    return pl.pallas_call(
        kernel,
        in_specs=[pl.BlockSpec(memory_space=pltpu.SMEM), vmem],
        out_specs=[vmem, vmem],
        out_shape=[half, half],
        name="first_coeffs",
        compiler_params=LARGE,
    )(where, init_coeffs)


def sum_and_fan(parts):
    n, half_k, sub = parts.shape

    def kernel(parts_ref, out_ref):
        acc = parts_ref[0].astype(jnp.float32)
        for i in range(1, n):
            acc = acc + parts_ref[i].astype(jnp.float32)
        acc = acc.astype(jnp.bfloat16)
        for i in range(2 * n):
            out_ref[i] = acc

    return pl.pallas_call(
        kernel, out_shape=jax.ShapeDtypeStruct((2 * n, half_k, sub), jnp.bfloat16), name="fan", compiler_params=SMALL
    )(parts)


def step_call(
    total,
    where,
    data,
    coeffs=None,
    grads=None,
    values=None,
    mixing=None,
    gathered=None,
    n_sub=None,
    rows=None,
    half_k=None,
):
    piece_rows, feats = data[0].shape
    n_pieces = len(data)
    pooled = n_pieces * piece_rows
    row_at, n_rows = rows
    comps = 2 * half_k
    low = jnp.bfloat16
    vmem, smem = pl.BlockSpec(memory_space=pltpu.VMEM), pl.BlockSpec(memory_space=pltpu.SMEM)
    args, specs, shapes = [where, *data], [smem] + [vmem] * n_pieces, []
    names = []

    def give(name, *arrays):
        for i, array in enumerate(arrays):
            names.append(f"{name}{i}")
            args.append(array)
            specs.append(vmem)

    if values is None:
        give("coeffs", *coeffs)
        if grads is not None:
            give("grads", *[term for pair in grads for term in pair])
            for i, one in enumerate(coeffs):
                shapes.append((f"new_coeffs{i}", jax.ShapeDtypeStruct(one.shape, jnp.float32)))
    else:
        give("values", values)
    if n_sub is not None:
        sub = pooled // n_sub
        shapes.append(("out_values", jax.ShapeDtypeStruct((n_rows, pooled), jnp.float32)))
        shapes.append(("parts", jax.ShapeDtypeStruct((n_sub, n_rows, sub), low)))
    if mixing is not None:
        give("mixing", mixing)
        give("gathered", gathered)
        shapes.append(("term", jax.ShapeDtypeStruct((n_rows, feats), low)))

    def kernel(where_ref, *refs):
        pieces = refs[:n_pieces]
        at = n_pieces
        ins = dict(zip(names, refs[at : at + len(names)], strict=True))
        at += len(names)
        outs = dict(zip([name for name, _ in shapes], refs[at : at + len(shapes)], strict=True))
        (resid,) = refs[at + len(shapes) :]
        base, core = where_ref[0], where_ref[1]

        def block_at(i):
            own = core if i % 2 == 0 else 1 - core
            return 2 * lax.bitwise_xor(base, i // 2) + own

        if mixing is not None:
            mixing_rows = ins["mixing0"][
                pl.ds(pl.multiple_of(core * half_k + row_at, n_rows), n_rows), :
            ]
            sub_in = gathered.shape[2]
            ratio = piece_rows // sub_in

            def set_resid(i, value):
                sums = [
                    gathered_block(ins["gathered0"], block_at(i) * ratio + r, comps)
                    for r in range(ratio)
                ]
                sums = sums[0] if ratio == 1 else jnp.concatenate(sums, axis=1)
                resid[:, pl.ds(i * piece_rows, piece_rows)] = (
                    value - mixed_dot(mixing_rows, sums)
                ).astype(low)

        if values is None:
            lows = []
            for i in range(len(coeffs)):
                weights = ins[f"coeffs{i}"][...]
                if grads is not None:
                    grad = ins[f"grads{2 * i}"][...].astype(jnp.float32)
                    grad = grad + ins[f"grads{2 * i + 1}"][...].astype(jnp.float32)
                    weights = weights - step_size * (grad / total + ridge_weight * weights)
                    outs[f"new_coeffs{i}"][...] = weights
                lows.append(weights.astype(low))
            weights = lows[0] if len(lows) == 1 else jnp.concatenate(lows, axis=0)
            for i in range(n_pieces):
                value = tall_dot(weights, pieces[i][...])
                if n_sub is not None:
                    outs["out_values"][:, pl.ds(i * piece_rows, piece_rows)] = value
                    ratio_out = piece_rows // sub
                    for r in range(ratio_out):
                        outs["parts"][block_at(i) * ratio_out + r] = value[
                            :, r * sub : (r + 1) * sub
                        ].astype(low)
                if mixing is not None:
                    set_resid(i, value)
        else:
            for i in range(n_pieces):
                set_resid(
                    i,
                    ins["values0"][
                        row_at : row_at + n_rows, pl.ds(i * piece_rows, piece_rows)
                    ],
                )
        if mixing is not None:
            wide = feats // 4
            for n in range(4):
                acc = None
                for i in range(n_pieces):
                    add = jnp.dot(
                        resid[:, pl.ds(i * piece_rows, piece_rows)],
                        pieces[i][:, pl.ds(n * wide, wide)],
                        preferred_element_type=jnp.float32,
                    )
                    acc = add if acc is None else acc + add
                outs["term"][:, pl.ds(n * wide, wide)] = acc.astype(low)

    return pl.pallas_call(
        kernel,
        in_specs=specs,
        out_specs=[vmem] * len(shapes),
        out_shape=[shape for _, shape in shapes],
        scratch_shapes=[
            pltpu.VMEM((n_rows, pooled), low),
        ],
        name="step",
        compiler_params=LARGE,
    )(*args)


class Grid:
    def __init__(self, n_view, n_samp):
        self.planes, self.squares = n_view // 2, n_samp // GROUP
        self.n_samp = n_samp

    def encode(self, plane, core, square, corner):
        return (plane * 2 + core) * self.n_samp + square * GROUP + corner

    def each(self):
        for plane in range(self.planes):
            for core in range(2):
                for square in range(self.squares):
                    for corner in range(GROUP):
                        yield plane, core, square, corner

    def permute(self, value, target):
        pairs = [(self.encode(*at), self.encode(*target(*at))) for at in self.each()]
        return lax.ppermute(value, AXES, pairs)

    def swap_core(self, value):
        return self.permute(value, lambda a, c, q, p: (a, 1 - c, q, p))

    def sum_squares(self, value, wire):
        low, other = value.astype(wire), jnp.zeros(value.shape, wire)
        bit = 1
        while bit < self.squares:
            if bit > 1:
                low = (low.astype(jnp.float32) + other.astype(jnp.float32)).astype(wire)
            other = self.permute(low, lambda a, c, q, p, bit=bit: (a, c, q ^ bit, p))
            bit *= 2
        return low, other

    def sum_planes(self, value):
        bit = 1
        while bit < self.planes:
            value = value + self.permute(value, lambda a, c, q, p, bit=bit: (a ^ bit, c, q, p))
            bit *= 2
        return value


def pick(parts, index):
    return lax.dynamic_index_in_dim(parts, index, 0, keepdims=False, allow_negative_indices=False)


def cut(value, start, size, axis):
    return lax.dynamic_slice_in_dim(value, start, size, axis, allow_negative_indices=False)


def pick(parts, index):
    return lax.dynamic_index_in_dim(parts, index, 0, keepdims=False, allow_negative_indices=False)


def cut(value, start, size, axis):
    return lax.dynamic_slice_in_dim(value, start, size, axis, allow_negative_indices=False)


def body(view_data, init_coeffs):
    low = jnp.bfloat16
    grid = Grid(lax.axis_size("view"), lax.axis_size("samp"))
    rows, feats = view_data.shape[1:]
    comps = init_coeffs.shape[2]
    half_k, half_rows = comps // 2, rows // 2
    total = rows * lax.axis_size("samp")
    n_sub = GROUP * grid.planes
    out_rows = feats // lax.axis_size("samp")
    view_at = lax.axis_index("view").astype(jnp.uint32)
    samp_at = lax.axis_index("samp").astype(jnp.uint32)
    core, other_core = view_at & 1, 1 - (view_at & 1)
    corner = samp_at & (GROUP - 1)
    base = 2 * core + (corner & 1)
    holder = (core == (corner >> 1)).astype(jnp.uint32)
    where = jnp.stack([base, core, corner * grid.planes, corner & 1]).astype(jnp.int32)
    pool_at = [((corner ^ k) & 1, ((corner ^ k) >> 1) * half_rows) for k in range(GROUP)]
    own_at, their_at = core * half_rows, other_core * half_rows
    out_at = [((samp_at & ~jnp.uint32(GROUP - 1)) + (base ^ k)) * out_rows for k in range(GROUP)]
    order_at = [corner ^ r for r in range(GROUP)]
    zero = jnp.uint32(0)
    held = (where, holder, pool_at, own_at, their_at, out_at, order_at)
    view_data, init_coeffs, held = lax.optimization_barrier((view_data, init_coeffs, held))
    where, holder, pool_at, own_at, their_at, out_at, order_at = held

    slots = [None] * GROUP

    def slice_piece(source, k):
        at = (*pool_at[k], zero)
        return lax.dynamic_slice(source, at, (1, half_rows, feats), allow_negative_indices=False)[0]

    early = [slice_piece(view_data, 1), slice_piece(view_data, 0)]
    view_later, *early = lax.optimization_barrier((view_data, *early))
    late = [slice_piece(view_later, 3), slice_piece(view_later, 2)]
    cut_pieces = {1: early[0], 0: early[1], 3: late[0], 2: late[1]}

    def pool(k):
        piece = cut_pieces[k]
        slots[k] = grid.permute(
            piece, lambda a, c, q, p, k=k: (a, (p ^ k) // 2, q, 2 * c + (p ^ k) % 2)
        )

    pool(1)
    pool(0)

    coeffs_low = init_coeffs.astype(low)
    part = jnp.zeros((comps, rows), jnp.float32)
    for member in range(view_data.shape[0]):
        part = part + lax.dot_general(
            coeffs_low[member],
            view_data[member],
            (((0,), (1,)), ((), ())),
            preferred_element_type=jnp.float32,
        )
    pool(3)
    pool(2)
    mine = cut(part, own_at, half_rows, 1)
    theirs = cut(part, their_at, half_rows, 1)
    mine = mine + grid.swap_core(theirs)
    mine = grid.sum_planes(mine)
    square_groups = [
        [grid.encode(a, c, q, p) for p in range(GROUP) for c in range(2)]
        for a in range(grid.planes)
        for q in range(grid.squares)
    ]
    gathered = lax.all_to_all(
        jnp.broadcast_to(mine.astype(low), (2 * GROUP, comps, half_rows)),
        AXES, 0, 0, axis_index_groups=square_groups,
    )
    coeffs, for_core = first_coeffs(init_coeffs, where)
    from_core = grid.swap_core(for_core)
    coeffs = jnp.where(holder == 1, coeffs, from_core)
    gathered, coeffs = lax.optimization_barrier((gathered, coeffs))

    shared_slots = {}
    for k in range(GROUP):
        shared_slots[k ^ 2] = grid.swap_core(slots[k])
    data = []
    for k in range(GROUP):
        data += [slots[k], shared_slots[k]]

    def gram_pair(gathered):
        return grid.sum_squares(gram_part(gathered, comps), jnp.float32)

    pair = gram_pair(gathered)
    mixing = newton_mixing(total, pair)

    reduce_groups = [
        [grid.encode(a, c, q, p) for p in range(GROUP) for a in range(grid.planes)]
        for c in range(2)
        for q in range(grid.squares)
    ]
    gather_groups = [
        [
            grid.encode(a, c, q, p)
            for c in range(2)
            for p in range(GROUP)
            for a in range(grid.planes)
        ]
        for q in range(grid.squares)
    ]
    n_rows = half_k // SETS
    values = None
    coeffs = [coeffs[n * n_rows : (n + 1) * n_rows] for n in range(SETS)]
    grads = [None] * SETS
    for outer_step in range(OUTER):
        given = {"mixing": mixing, "gathered": gathered, "half_k": half_k}
        for inner_step in range(INNER):
            for n in range(SETS):
                rows_of = (n * n_rows, n_rows)
                if inner_step == 0 and outer_step > 0:
                    (term,) = step_call(total, where, data, values=values, rows=rows_of, **given)
                elif grads[n] is None:
                    (term,) = step_call(
                        total, where, data, coeffs=[coeffs[n]], rows=rows_of, **given
                    )
                else:
                    coeffs[n], term = step_call(
                        total,
                        where,
                        data,
                        coeffs=[coeffs[n]],
                        grads=[grads[n]],
                        rows=rows_of,
                        **given,
                    )
                grads[n] = grid.sum_squares(term, low)
        *coeffs, values, parts = step_call(
            total,
            where,
            data,
            coeffs=coeffs,
            grads=grads,
            n_sub=n_sub,
            rows=(0, half_k),
            half_k=half_k,
        )
        grads = [None] * SETS
        parts = lax.all_to_all(parts, AXES, 0, 0, axis_index_groups=reduce_groups)
        gathered = lax.all_to_all(sum_and_fan(parts), AXES, 0, 0, axis_index_groups=gather_groups)
        if outer_step < OUTER - 1:
            mixing = newton_mixing(total, gram_pair(gathered))
    pair = gram_pair(gathered)
    shared = newton_scores(total, pair, gathered, where, grid.planes)

    pieces = []
    for k in range(GROUP):
        piece = jnp.concatenate([cut(one, out_at[k], out_rows, 1) for one in coeffs], axis=0)
        pieces.append(
            grid.permute(
                piece,
                lambda a, c, q, p, k=k: (a, p // 2, q, (2 * c + p % 2) ^ k),
            )
        )
    pieces = jnp.stack(pieces)
    ordered = [pick(pieces, order_at[r]) for r in range(GROUP)]
    final = jnp.stack(
        [jnp.concatenate([ordered[member], ordered[2 + member]], axis=0).T for member in range(2)]
    )
    return (shared, final)


def solution(mesh):
    in_specs = (P("view", "samp", None), P("view", None, None))
    out_specs = (P("samp", None), P("view", "samp", None))

    return jax.shard_map(body, mesh=mesh, in_specs=in_specs, out_specs=out_specs, check_vma=False)
```

```python
import jax
import jax.numpy as jnp
from jax import lax
from jax.experimental import pallas as pl
from jax.experimental.pallas import tpu as pltpu
from jax.sharding import PartitionSpec as P


OUTER = 2
INNER = 2
NS_ITERS = 12

ridge_weight = 0.1
step_size = 0.5
AXES = ("view", "samp")
SETS = 2
GROUP = 4

SMALL = pltpu.CompilerParams(vmem_limit_bytes=4 << 20)
LARGE = pltpu.CompilerParams(vmem_limit_bytes=16 << 20)


def split(value):
    top = value.astype(jnp.bfloat16)
    return top, (value - top.astype(jnp.float32)).astype(jnp.bfloat16)


def fine_dot(left, right):
    left_top, left_rest = split(left)
    right_top, right_rest = split(right)
    out = jnp.dot(left_top, right_rest, preferred_element_type=jnp.float32)
    out = out + jnp.dot(left_rest, right_top, preferred_element_type=jnp.float32)
    return out + jnp.dot(left_top, right_top, preferred_element_type=jnp.float32)


def tall_dot(left, right):
    return lax.dot_general(left, right, (((1,), (1,)), ((), ())), preferred_element_type=jnp.float32)


def mixed_dot(mixing, sums):
    top, rest = split(mixing)
    return jnp.dot(rest, sums, preferred_element_type=jnp.float32) + jnp.dot(
        top, sums, preferred_element_type=jnp.float32
    )


def newton(total, gram):
    size_k = gram.shape[0]
    row = lax.broadcasted_iota(jnp.int32, gram.shape, 0)
    col = lax.broadcasted_iota(jnp.int32, gram.shape, 1)
    eye_mat = jnp.where(row == col, 1.0, 0.0)

    def whole_sum(value):
        return jnp.sum(jnp.sum(value, axis=0, keepdims=True), axis=1, keepdims=True)

    shrunk = gram + whole_sum(gram * eye_mat) / size_k * eye_mat
    scale = jnp.sqrt(whole_sum(shrunk * shrunk))
    approx = shrunk / scale
    inverse = 0.5 * (3.0 * eye_mat - approx)
    approx = fine_dot(approx, inverse)

    def turn(_, state):
        approx, inverse = state
        factor = 0.5 * (3.0 * eye_mat - fine_dot(inverse, approx))
        stacked = fine_dot(jnp.concatenate([approx, inverse], axis=0), factor)
        return stacked[:size_k], stacked[size_k:]

    approx, inverse = lax.fori_loop(1, NS_ITERS - 1, turn, (approx, inverse), unroll=5)
    factor = 0.5 * (3.0 * eye_mat - fine_dot(inverse, approx))
    inverse = fine_dot(inverse, factor)
    return inverse * jnp.sqrt(total / scale)


def gathered_block(gathered_ref, index, comps):
    if gathered_ref.shape[1] == comps:
        return gathered_ref[index]
    half = gathered_ref.shape[0] // 2
    return jnp.concatenate([gathered_ref[index], gathered_ref[half + index]], axis=0)


def newton_mixing(total, pair):
    def kernel(part_ref, other_ref, mixing_ref):
        mixing_ref[...] = newton(total, part_ref[...] + other_ref[...])

    return pl.pallas_call(
        kernel, out_shape=jax.ShapeDtypeStruct(pair[0].shape, jnp.float32), name="newton", compiler_params=SMALL
    )(*pair)


def newton_scores(total, pair, gathered, where, n_blocks):
    comps, sub = pair[0].shape[0], gathered.shape[2]

    def kernel(where_ref, part_ref, other_ref, gathered_ref, out_ref):
        mixing = newton(total, part_ref[...] + other_ref[...])
        for n in range(n_blocks):
            sums = gathered_block(gathered_ref, where_ref[2] + n, comps)
            out_ref[pl.ds(n * sub, sub), :] = mixed_dot(mixing, sums).T

    vmem = pl.BlockSpec(memory_space=pltpu.VMEM)
    return pl.pallas_call(
        kernel,
        in_specs=[pl.BlockSpec(memory_space=pltpu.SMEM), vmem, vmem, vmem],
        out_specs=vmem,
        out_shape=jax.ShapeDtypeStruct((n_blocks * sub, comps), jnp.float32),
        name="newton_scores",
        compiler_params=SMALL,
    )(where, *pair, gathered)


def gram_part(gathered, comps):
    count = gathered.shape[0] * gathered.shape[1] // comps

    def kernel(gathered_ref, out_ref):
        acc = None
        for n in range(count):
            sums = gathered_block(gathered_ref, n, comps)
            add = tall_dot(sums, sums)
            acc = add if acc is None else acc + add
        out_ref[...] = acc

    return pl.pallas_call(
        kernel,
        out_shape=jax.ShapeDtypeStruct((comps, comps), jnp.float32),
        name="gram",
        compiler_params=SMALL,
    )(gathered)


def first_coeffs(init_coeffs, where):
    _, feats, comps = init_coeffs.shape
    half_k = comps // 2

    def kernel(where_ref, init_ref, own_ref, other_ref):
        turned = init_ref[where_ref[3]].T
        first, second = turned[:half_k], turned[half_k:]
        swap = where_ref[1] == 1
        own_ref[...] = jnp.where(swap, second, first)
        other_ref[...] = jnp.where(swap, first, second)

    vmem = pl.BlockSpec(memory_space=pltpu.VMEM)
    half = jax.ShapeDtypeStruct((half_k, feats), jnp.float32)
    return pl.pallas_call(
        kernel,
        in_specs=[pl.BlockSpec(memory_space=pltpu.SMEM), vmem],
        out_specs=[vmem, vmem],
        out_shape=[half, half],
        name="first_coeffs",
        compiler_params=LARGE,
    )(where, init_coeffs)


def sum_and_fan(parts):
    n, half_k, sub = parts.shape

    def kernel(parts_ref, out_ref):
        acc = parts_ref[0].astype(jnp.float32)
        for i in range(1, n):
            acc = acc + parts_ref[i].astype(jnp.float32)
        acc = acc.astype(jnp.bfloat16)
        for i in range(2 * n):
            out_ref[i] = acc

    return pl.pallas_call(
        kernel, out_shape=jax.ShapeDtypeStruct((2 * n, half_k, sub), jnp.bfloat16), name="fan", compiler_params=SMALL
    )(parts)


def step_call(
    total,
    where,
    data,
    coeffs=None,
    grads=None,
    values=None,
    mixing=None,
    gathered=None,
    n_sub=None,
    rows=None,
    half_k=None,
):
    piece_rows, feats = data[0].shape
    n_pieces = len(data)
    pooled = n_pieces * piece_rows
    row_at, n_rows = rows
    comps = 2 * half_k
    low = jnp.bfloat16
    vmem, smem = pl.BlockSpec(memory_space=pltpu.VMEM), pl.BlockSpec(memory_space=pltpu.SMEM)
    args, specs, shapes = [where, *data], [smem] + [vmem] * n_pieces, []
    names = []

    def give(name, *arrays):
        for i, array in enumerate(arrays):
            names.append(f"{name}{i}")
            args.append(array)
            specs.append(vmem)

    if values is None:
        give("coeffs", *coeffs)
        if grads is not None:
            give("grads", *[term for pair in grads for term in pair])
            for i, one in enumerate(coeffs):
                shapes.append((f"new_coeffs{i}", jax.ShapeDtypeStruct(one.shape, jnp.float32)))
    else:
        give("values", values)
    if n_sub is not None:
        sub = pooled // n_sub
        shapes.append(("out_values", jax.ShapeDtypeStruct((n_rows, pooled), jnp.float32)))
        shapes.append(("parts", jax.ShapeDtypeStruct((n_sub, n_rows, sub), low)))
    if mixing is not None:
        give("mixing", mixing)
        give("gathered", gathered)
        shapes.append(("term", jax.ShapeDtypeStruct((n_rows, feats), low)))

    def kernel(where_ref, *refs):
        pieces = refs[:n_pieces]
        at = n_pieces
        ins = dict(zip(names, refs[at : at + len(names)], strict=True))
        at += len(names)
        outs = dict(zip([name for name, _ in shapes], refs[at : at + len(shapes)], strict=True))
        (resid,) = refs[at + len(shapes) :]
        base, core = where_ref[0], where_ref[1]

        def block_at(i):
            own = core if i % 2 == 0 else 1 - core
            return 2 * lax.bitwise_xor(base, i // 2) + own

        if mixing is not None:
            mixing_rows = ins["mixing0"][
                pl.ds(pl.multiple_of(core * half_k + row_at, n_rows), n_rows), :
            ]
            sub_in = gathered.shape[2]
            ratio = piece_rows // sub_in

            def set_resid(i, value):
                sums = [
                    gathered_block(ins["gathered0"], block_at(i) * ratio + r, comps)
                    for r in range(ratio)
                ]
                sums = sums[0] if ratio == 1 else jnp.concatenate(sums, axis=1)
                resid[:, pl.ds(i * piece_rows, piece_rows)] = (
                    value - mixed_dot(mixing_rows, sums)
                ).astype(low)

        if values is None:
            lows = []
            for i in range(len(coeffs)):
                weights = ins[f"coeffs{i}"][...]
                if grads is not None:
                    grad = ins[f"grads{2 * i}"][...].astype(jnp.float32)
                    grad = grad + ins[f"grads{2 * i + 1}"][...].astype(jnp.float32)
                    weights = weights - step_size * (grad / total + ridge_weight * weights)
                    outs[f"new_coeffs{i}"][...] = weights
                lows.append(weights.astype(low))
            weights = lows[0] if len(lows) == 1 else jnp.concatenate(lows, axis=0)
            for i in range(n_pieces):
                value = tall_dot(weights, pieces[i][...])
                if n_sub is not None:
                    outs["out_values"][:, pl.ds(i * piece_rows, piece_rows)] = value
                    ratio_out = piece_rows // sub
                    for r in range(ratio_out):
                        outs["parts"][block_at(i) * ratio_out + r] = value[
                            :, r * sub : (r + 1) * sub
                        ].astype(low)
                if mixing is not None:
                    set_resid(i, value)
        else:
            for i in range(n_pieces):
                set_resid(
                    i,
                    ins["values0"][
                        row_at : row_at + n_rows, pl.ds(i * piece_rows, piece_rows)
                    ],
                )
        if mixing is not None:
            wide = feats // 4
            for n in range(4):
                acc = None
                for i in range(n_pieces):
                    add = jnp.dot(
                        resid[:, pl.ds(i * piece_rows, piece_rows)],
                        pieces[i][:, pl.ds(n * wide, wide)],
                        preferred_element_type=jnp.float32,
                    )
                    acc = add if acc is None else acc + add
                outs["term"][:, pl.ds(n * wide, wide)] = acc.astype(low)

    return pl.pallas_call(
        kernel,
        in_specs=specs,
        out_specs=[vmem] * len(shapes),
        out_shape=[shape for _, shape in shapes],
        scratch_shapes=[
            pltpu.VMEM((n_rows, pooled), low),
        ],
        name="step",
        compiler_params=LARGE,
    )(*args)


class Grid:
    def __init__(self, n_view, n_samp):
        self.planes, self.squares = n_view // 2, n_samp // GROUP
        self.n_samp = n_samp

    def encode(self, plane, core, square, corner):
        return (plane * 2 + core) * self.n_samp + square * GROUP + corner

    def each(self):
        for plane in range(self.planes):
            for core in range(2):
                for square in range(self.squares):
                    for corner in range(GROUP):
                        yield plane, core, square, corner

    def permute(self, value, target):
        pairs = [(self.encode(*at), self.encode(*target(*at))) for at in self.each()]
        return lax.ppermute(value, AXES, pairs)

    def swap_core(self, value):
        return self.permute(value, lambda a, c, q, p: (a, 1 - c, q, p))

    def sum_squares(self, value, wire):
        low, other = value.astype(wire), jnp.zeros(value.shape, wire)
        bit = 1
        while bit < self.squares:
            if bit > 1:
                low = (low.astype(jnp.float32) + other.astype(jnp.float32)).astype(wire)
            other = self.permute(low, lambda a, c, q, p, bit=bit: (a, c, q ^ bit, p))
            bit *= 2
        return low, other

    def sum_planes(self, value):
        bit = 1
        while bit < self.planes:
            value = value + self.permute(value, lambda a, c, q, p, bit=bit: (a ^ bit, c, q, p))
            bit *= 2
        return value


def pick(parts, index):
    return lax.dynamic_index_in_dim(parts, index, 0, keepdims=False, allow_negative_indices=False)


def cut(value, start, size, axis):
    return lax.dynamic_slice_in_dim(value, start, size, axis, allow_negative_indices=False)


def pick(parts, index):
    return lax.dynamic_index_in_dim(parts, index, 0, keepdims=False, allow_negative_indices=False)


def cut(value, start, size, axis):
    return lax.dynamic_slice_in_dim(value, start, size, axis, allow_negative_indices=False)


def body(view_data, init_coeffs):
    low = jnp.bfloat16
    grid = Grid(lax.axis_size("view"), lax.axis_size("samp"))
    rows, feats = view_data.shape[1:]
    comps = init_coeffs.shape[2]
    half_k, half_rows = comps // 2, rows // 2
    total = rows * lax.axis_size("samp")
    n_sub = GROUP * grid.planes
    out_rows = feats // lax.axis_size("samp")
    view_at = lax.axis_index("view").astype(jnp.uint32)
    samp_at = lax.axis_index("samp").astype(jnp.uint32)
    core, other_core = view_at & 1, 1 - (view_at & 1)
    corner = samp_at & (GROUP - 1)
    base = 2 * core + (corner & 1)
    holder = (core == (corner >> 1)).astype(jnp.uint32)
    where = jnp.stack([base, core, corner * grid.planes, corner & 1]).astype(jnp.int32)
    pool_at = [((corner ^ k) & 1, ((corner ^ k) >> 1) * half_rows) for k in range(GROUP)]
    own_at, their_at = core * half_rows, other_core * half_rows
    out_at = [((samp_at & ~jnp.uint32(GROUP - 1)) + (base ^ k)) * out_rows for k in range(GROUP)]
    order_at = [corner ^ r for r in range(GROUP)]
    zero = jnp.uint32(0)
    held = (where, holder, pool_at, own_at, their_at, out_at, order_at)
    view_data, init_coeffs, held = lax.optimization_barrier((view_data, init_coeffs, held))
    where, holder, pool_at, own_at, their_at, out_at, order_at = held

    slots = [None] * GROUP

    def slice_piece(source, k):
        at = (*pool_at[k], zero)
        return lax.dynamic_slice(source, at, (1, half_rows, feats), allow_negative_indices=False)[0]

    early = [slice_piece(view_data, 1)]
    view_later, early[0] = lax.optimization_barrier((view_data, early[0]))
    early.append(slice_piece(view_later, 0))
    view_later, early[1] = lax.optimization_barrier((view_later, early[1]))
    late = [slice_piece(view_later, 3), slice_piece(view_later, 2)]
    cut_pieces = {1: early[0], 0: early[1], 3: late[0], 2: late[1]}

    def pool(k):
        piece = cut_pieces[k]
        slots[k] = grid.permute(
            piece, lambda a, c, q, p, k=k: (a, (p ^ k) // 2, q, 2 * c + (p ^ k) % 2)
        )

    pool(1)
    pool(0)

    coeffs_low = init_coeffs.astype(low)
    part = jnp.zeros((comps, rows), jnp.float32)
    for member in range(view_data.shape[0]):
        part = part + lax.dot_general(
            coeffs_low[member],
            view_data[member],
            (((0,), (1,)), ((), ())),
            preferred_element_type=jnp.float32,
        )
    pool(3)
    pool(2)
    mine = cut(part, own_at, half_rows, 1)
    theirs = cut(part, their_at, half_rows, 1)
    mine = mine + grid.swap_core(theirs)
    mine = grid.sum_planes(mine)
    square_groups = [
        [grid.encode(a, c, q, p) for p in range(GROUP) for c in range(2)]
        for a in range(grid.planes)
        for q in range(grid.squares)
    ]
    gathered = lax.all_to_all(
        jnp.broadcast_to(mine.astype(low), (2 * GROUP, comps, half_rows)),
        AXES, 0, 0, axis_index_groups=square_groups,
    )
    coeffs, for_core = first_coeffs(init_coeffs, where)
    from_core = grid.swap_core(for_core)
    coeffs = jnp.where(holder == 1, coeffs, from_core)
    n_rows = half_k // SETS
    coeffs = [coeffs[n * n_rows : (n + 1) * n_rows] for n in range(SETS)]
    gathered, *coeffs = lax.optimization_barrier((gathered, *coeffs))

    shared_slots = {}
    for k in range(GROUP):
        shared_slots[k ^ 2] = grid.swap_core(slots[k])
    data = []
    for k in range(GROUP):
        data += [slots[k], shared_slots[k]]

    def gram_pair(gathered):
        return grid.sum_squares(gram_part(gathered, comps), jnp.float32)

    pair = gram_pair(gathered)
    mixing = newton_mixing(total, pair)

    reduce_groups = [
        [grid.encode(a, c, q, p) for p in range(GROUP) for a in range(grid.planes)]
        for c in range(2)
        for q in range(grid.squares)
    ]
    gather_groups = [
        [
            grid.encode(a, c, q, p)
            for c in range(2)
            for p in range(GROUP)
            for a in range(grid.planes)
        ]
        for q in range(grid.squares)
    ]
    values = None
    grads = [None] * SETS
    for outer_step in range(OUTER):
        given = {"mixing": mixing, "gathered": gathered, "half_k": half_k}
        for inner_step in range(INNER):
            for n in range(SETS):
                rows_of = (n * n_rows, n_rows)
                if inner_step == 0 and outer_step > 0:
                    (term,) = step_call(total, where, data, values=values, rows=rows_of, **given)
                elif grads[n] is None:
                    (term,) = step_call(
                        total, where, data, coeffs=[coeffs[n]], rows=rows_of, **given
                    )
                else:
                    coeffs[n], term = step_call(
                        total,
                        where,
                        data,
                        coeffs=[coeffs[n]],
                        grads=[grads[n]],
                        rows=rows_of,
                        **given,
                    )
                grads[n] = grid.sum_squares(term, low)
        *coeffs, values, parts = step_call(
            total,
            where,
            data,
            coeffs=coeffs,
            grads=grads,
            n_sub=n_sub,
            rows=(0, half_k),
            half_k=half_k,
        )
        grads = [None] * SETS
        parts = lax.all_to_all(parts, AXES, 0, 0, axis_index_groups=reduce_groups)
        gathered = lax.all_to_all(sum_and_fan(parts), AXES, 0, 0, axis_index_groups=gather_groups)
        if outer_step < OUTER - 1:
            mixing = newton_mixing(total, gram_pair(gathered))
    pair = gram_pair(gathered)
    shared = newton_scores(total, pair, gathered, where, grid.planes)

    pieces = []
    for k in range(GROUP):
        piece = jnp.concatenate([cut(one, out_at[k], out_rows, 1) for one in coeffs], axis=0)
        pieces.append(
            grid.permute(
                piece,
                lambda a, c, q, p, k=k: (a, p // 2, q, (2 * c + p % 2) ^ k),
            )
        )
    pieces = jnp.stack(pieces)
    ordered = [pick(pieces, order_at[r]) for r in range(GROUP)]
    final = jnp.stack(
        [jnp.concatenate([ordered[member], ordered[2 + member]], axis=0).T for member in range(2)]
    )
    return (shared, final)


def solution(mesh):
    in_specs = (P("view", "samp", None), P("view", None, None))
    out_specs = (P("samp", None), P("view", "samp", None))

    return jax.shard_map(body, mesh=mesh, in_specs=in_specs, out_specs=out_specs, check_vma=False)
```
